128 devices in a mesh: blk: 128 (over z, x, y, core).
Axes of the slice: x: 4, y: 4, z: 4, core: 2. Of those that a mesh axis runs over, the one named last changes fastest.
Arguments:
- single: bfloat16 [2048, 384], P('blk'), may hold values from -6 to 6
- angles: float32 [3, 2048], P(None, 'blk'), may hold values from -3.140625 to 3.140625
- trans: float32 [3, 2048], P(None, 'blk'), may hold values from -6 to 6
- left_factor: bfloat16 [2048, 64], P('blk'), may hold values from -6 to 6
- right_factor: bfloat16 [2048, 64], P('blk'), may hold values from -6 to 6
- chain: int32 [2048], P('blk'), may hold values from 0 to 7, never falling along the last dimension, each value on 1 to 512 neighbouring positions
- live: int32 [2048], P('blk'), may hold values 0 or 1
- w_query: bfloat16 [384, 192], replicated, may hold values from -0.3125 to 0.3125
- w_keyval: bfloat16 [384, 384], replicated, may hold values from -0.3125 to 0.3125
- w_qpoints: bfloat16 [384, 144], replicated, may hold values from -0.3125 to 0.3125
- w_kvpoints: bfloat16 [384, 432], replicated, may hold values from -0.3125 to 0.3125
- w_pair_in: bfloat16 [64, 128], replicated, may hold values from -0.75 to 0.75
- chain_bias: float32 [128], replicated, may hold values from -6 to 6
- w_pair_out: bfloat16 [128, 128], replicated, may hold values from -0.5 to 0.5
- w_bias: bfloat16 [128, 12], replicated, may hold values from -0.5 to 0.5
- point_weight: float32 [12], replicated, may hold values from 0.1 to 1
- w_out: bfloat16 [2112, 384], replicated, may hold values from -0.125 to 0.125
- out_gain: float32 [384], replicated, may hold values from 0.5 to 1.5
- w_frame: float32 [384, 6], replicated, may hold values from -0.3125 to 0.3125
Outputs:
- single_out: bfloat16 [2048, 384], P('blk')
- frames_out: float32 [12, 2048], P(None, 'blk')
The draws below stay inside these ranges and needn't reach their ends.
Inputs may be any that keep to these rules, and one draw needn't show every extreme that they name: Residues of one chain are consecutive and chain numbers never fall along the residues; a chain has 1 to 512 residues.
All inputs are finite; a program needn't handle non-finite values. No bound on the sum of `live` on one device may be relied on, other than what follows from the above.
Results may differ from the reference program's by a relative error of at most 0.0035.
Values may be sent and summed in bfloat16 or wider, within the bound.
No kernel may reach another device: no remote copies, remote signals or barrier semaphores. Data moves between devices by JAX's collectives and lax.ppermute only.
A program may use at most 192 MiB of HBM per device.

```python
import math
import jax
import jax.numpy as jnp
import numpy as np
from jax import lax

CS = 384
HEADS = 12
HEAD_DIM = 16
QPTS = 4
VPTS = 8
CZ = 128
RANK = 64
CHAINS = 8
RES_DEV = 16
RES = 2048
N_BLK = 128


def place_ends(result, rng, smallest, largest):
    index_at = [jax.random.randint(jax.random.fold_in(rng, axis), (), 0, length) for axis, length in enumerate(result.shape)]
    main_axis = result.shape.index(max(result.shape))
    beside = index_at[:main_axis] + [(index_at[main_axis] + 1) % result.shape[main_axis]] + index_at[main_axis + 1:]
    return result.at[tuple(index_at)].set(smallest).at[tuple(beside)].set(largest)


def block_levels(stream_key, shape, split, smallest, top_value):
    level = 1.0
    for position, blocks in split:
        draws = jax.random.uniform(jax.random.fold_in(jax.random.fold_in(stream_key, 6), position), (blocks,), jnp.float32, smallest / len(split), top_value / len(split))
        level = level * jnp.repeat(jnp.exp(draws), shape[position] // blocks).reshape((-1,) + (1,) * (len(shape) - 1 - position))
    return level


def length_profile(amount, total, bound, skew):
    portions = [(1 << 20) // math.isqrt(standing ** skew) + 1 for standing in range(2, amount + 1)]
    rest, given = total - bound - (amount - 1), [1] * (amount - 1)
    while rest > 0:
        free = [i for i in range(amount - 1) if given[i] < bound]
        pool, remaining = sum([portions[i] for i in free]), rest
        for i in free:
            more = min(bound - given[i], max(1, remaining * portions[i] // pool), rest)
            given[i] = given[i] + more
            rest = rest - more
    return np.array([bound] + given)


def ragged_sizes(stream_key, amount, total, reach, slope):
    if amount == 2:
        one = jax.random.randint(stream_key, (), max(1, total - reach), min(reach, total - 1) + 1)
        return jnp.stack([one, total - one])
    sizes = jnp.asarray(length_profile(amount, total, reach, slope), jnp.int32)
    twos = (amount - 1) // 2
    source_of, taker = sizes[1:1 + 2 * twos:2], sizes[2:2 + 2 * twos:2]
    slack = jnp.minimum(source_of - 1, reach - taker)
    moved = jax.random.randint(jax.random.fold_in(stream_key, 1), (twos,), 0, 1 << 20) % (slack + 1)
    sizes = sizes.at[1:1 + 2 * twos:2].set(source_of - moved).at[2:2 + 2 * twos:2].set(taker + moved)
    return sizes[jax.random.permutation(jax.random.fold_in(stream_key, 2), amount)]


def bell_draw(key, shape, scale, limit, split=(), kind=jnp.bfloat16):
    entries = jax.random.normal(key, shape, jnp.float32) * scale
    if len(split) > 0:
        entries = block_levels(key, shape, split, -0.22, 0.18) * entries
    return jnp.clip(entries, min=-limit, max=limit).astype(kind)


def setup_inputs(seed: int = 0) -> dict:
    streams_of = jax.random.split(jax.random.key(seed), 20)
    return {
        "single": bell_draw(streams_of[0], (RES, CS), 1.0, 6.0, ((0, 128),)),
        "angles": jnp.clip(jax.random.uniform(streams_of[1], (3, RES), jnp.float32, -3.140625, 3.140625), -3.140625, 3.140625),
        "trans": bell_draw(streams_of[2], (3, RES), 1.0, 6.0, ((1, 128),), jnp.float32),
        "left_factor": bell_draw(streams_of[3], (RES, RANK), 1.0, 6.0, ((0, 128),)),
        "right_factor": bell_draw(streams_of[4], (RES, RANK), 1.0, 6.0, ((0, 128),)),
        "chain": jnp.searchsorted(jnp.cumsum(ragged_sizes(streams_of[5], CHAINS, RES, RES // 4, 0)), jnp.arange(RES), side="right").astype(jnp.int32),
        "live": place_ends((jax.random.randint(streams_of[6], (RES,), 0, 16) < 15).astype(jnp.int32), jax.random.fold_in(streams_of[6], 1), 0, 1),
        "w_query": bell_draw(streams_of[7], (CS, HEADS * HEAD_DIM), CS ** -0.5, 0.3125),
        "w_keyval": bell_draw(streams_of[8], (CS, 2 * HEADS * HEAD_DIM), CS ** -0.5, 0.3125),
        "w_qpoints": bell_draw(streams_of[9], (CS, 3 * HEADS * QPTS), CS ** -0.5, 0.3125),
        "w_kvpoints": bell_draw(streams_of[10], (CS, 3 * HEADS * (QPTS + VPTS)), CS ** -0.5, 0.3125),
        "w_pair_in": bell_draw(streams_of[11], (RANK, CZ), RANK ** -0.5, 0.75),
        "chain_bias": bell_draw(streams_of[12], (CZ,), 1.0, 6.0, (), jnp.float32),
        "w_pair_out": bell_draw(streams_of[13], (CZ, CZ), CZ ** -0.5, 0.5),
        "w_bias": bell_draw(streams_of[14], (CZ, HEADS), CZ ** -0.5, 0.5),
        "point_weight": jnp.clip(jnp.exp(jax.random.uniform(streams_of[15], (HEADS,), jnp.float32, math.log(0.1), math.log(1.0))), 0.1, 1.0),
        "w_out": bell_draw(streams_of[16], (HEADS * (HEAD_DIM + 4 * VPTS + CZ), CS), (HEADS * (HEAD_DIM + 4 * VPTS + CZ)) ** -0.5, 0.125),
        "out_gain": jnp.clip(1.0 + 0.1 * jax.random.normal(streams_of[17], (CS,), jnp.float32), 0.5, 1.5),
        "w_frame": bell_draw(streams_of[18], (CS, 6), CS ** -0.5, 0.3125, (), jnp.float32),
    }


def mm(form, left, right):
    return jnp.einsum(form, left.astype(jnp.float32), right.astype(jnp.float32), precision=lax.Precision.HIGHEST)

def rotation(angles):
    ca, sa = (jnp.cos(angles[0]), jnp.sin(angles[0]))
    cb, sb = (jnp.cos(angles[1]), jnp.sin(angles[1]))
    cc, sc = (jnp.cos(angles[2]), jnp.sin(angles[2]))
    first = jnp.stack([ca * cb, -sa * cc + ca * sb * sc, sa * sc + ca * sb * cc])
    second = jnp.stack([sa * cb, ca * cc + sa * sb * sc, -ca * sc + sa * sb * cc])
    third = jnp.stack([-sb, cb * sc, cb * cc])
    return jnp.stack([first, second, third])

def quat_rotation(bpart, cpart, dpart):
    norm = jnp.sqrt(1.0 + bpart * bpart + cpart * cpart + dpart * dpart)
    apart = 1.0 / norm
    bpart, cpart, dpart = (bpart / norm, cpart / norm, dpart / norm)
    first = jnp.stack([apart * apart + bpart * bpart - cpart * cpart - dpart * dpart, 2.0 * (bpart * cpart - apart * dpart), 2.0 * (bpart * dpart + apart * cpart)])
    second = jnp.stack([2.0 * (bpart * cpart + apart * dpart), apart * apart - bpart * bpart + cpart * cpart - dpart * dpart, 2.0 * (cpart * dpart - apart * bpart)])
    third = jnp.stack([2.0 * (bpart * dpart - apart * cpart), 2.0 * (cpart * dpart + apart * bpart), apart * apart - bpart * bpart - cpart * cpart + dpart * dpart])
    return jnp.stack([first, second, third])

def to_global(rot, shift, points):
    return jnp.einsum('xyn,nyhp->nxhp', rot, points, precision=lax.Precision.HIGHEST) + shift.T[:, :, None, None]

def pair_features(left, right, same, w_pair_in, chain_bias, w_pair_out):
    prod = (left.astype(jnp.float32)[:, None, :] * right.astype(jnp.float32)[None, :, :]).astype(jnp.bfloat16)
    hidden = mm('qkr,rz->qkz', prod, w_pair_in) + same[:, :, None] * chain_bias
    hidden = jax.nn.gelu(hidden, approximate=True).astype(jnp.bfloat16)
    outer = mm('qkz,zy->qky', hidden, w_pair_out)
    center = outer - lax.optimization_barrier(jnp.mean(outer, axis=2, keepdims=True))
    spread = lax.optimization_barrier(jnp.mean(center * center, axis=2, keepdims=True))
    return (center * lax.rsqrt(spread + 1e-05)).astype(jnp.bfloat16)

def reference(single, angles, trans, left_factor, right_factor, chain, live, w_query, w_keyval, w_qpoints, w_kvpoints, w_pair_in, chain_bias, w_pair_out, w_bias, point_weight, w_out, out_gain, w_frame):
    width = HEADS * HEAD_DIM
    rot = rotation(angles)
    keyval = jnp.dot(single, w_keyval, preferred_element_type=jnp.float32).astype(jnp.bfloat16)
    keys = keyval[:, :width].reshape(RES, HEADS, HEAD_DIM)
    values = keyval[:, width:].reshape(RES, HEADS, HEAD_DIM)
    kvpoints = jnp.dot(single, w_kvpoints, preferred_element_type=jnp.float32).reshape(RES, 3, HEADS, QPTS + VPTS)
    kvglobal = to_global(rot, trans, kvpoints).astype(jnp.bfloat16)
    kglobal = kvglobal[..., :QPTS].astype(jnp.float32)
    vglobal = kvglobal[..., QPTS:]
    ksq = lax.optimization_barrier(jnp.sum(kglobal * kglobal, axis=(1, 3))).T
    coef = point_weight * (2.0 / (9.0 * QPTS)) ** 0.5 / 2.0
    dead = 100000.0 * (1.0 - live.astype(jnp.float32))

    def one_block(index):
        start = index * RES_DEV
        rows = lax.dynamic_slice_in_dim(single, start, RES_DEV, 0)
        rot_rows = lax.dynamic_slice_in_dim(rot, start, RES_DEV, 2)
        trans_rows = lax.dynamic_slice_in_dim(trans, start, RES_DEV, 1)
        left_rows = lax.dynamic_slice_in_dim(left_factor, start, RES_DEV, 0)
        chain_rows = lax.dynamic_slice_in_dim(chain, start, RES_DEV, 0)
        query = jnp.dot(rows, w_query, preferred_element_type=jnp.float32).astype(jnp.bfloat16).reshape(RES_DEV, HEADS, HEAD_DIM)
        qpoints = jnp.dot(rows, w_qpoints, preferred_element_type=jnp.float32).reshape(RES_DEV, 3, HEADS, QPTS)
        qglobal = to_global(rot_rows, trans_rows, qpoints)
        qsq = lax.optimization_barrier(jnp.sum(qglobal * qglobal, axis=(1, 3))).T
        same = (chain_rows[:, None] == chain[None, :]).astype(jnp.float32)
        pair = pair_features(left_rows, right_factor, same, w_pair_in, chain_bias, w_pair_out)
        scalar = mm('qhc,khc->hqk', query, keys) * HEAD_DIM ** (-0.5)
        bias = mm('qkz,zh->hqk', pair, w_bias)
        cross = mm('qxhp,kxhp->hqk', qglobal, kglobal)
        dist = qsq[:, :, None] + ksq[:, None, :] - 2.0 * cross
        logits = (1.0 / 3.0) ** 0.5 * (scalar + bias - coef[:, None, None] * dist) - dead[None, None, :]
        top = lax.optimization_barrier(jnp.max(logits, axis=2, keepdims=True))
        terms = jnp.exp(logits - top)
        total = lax.optimization_barrier(jnp.sum(terms, axis=2))
        weights = terms.astype(jnp.bfloat16)
        att_values = mm('hqk,khc->hqc', weights, values) / total[:, :, None]
        att_points = mm('hqk,kxhp->hqxp', weights, vglobal) / total[:, :, None, None]
        att_pair = mm('hqk,qkz->hqz', weights, pair) / total[:, :, None]
        local = jnp.einsum('yxq,hqyp->hqxp', rot_rows, att_points - trans_rows.T[None, :, :, None], precision=lax.Precision.HIGHEST)
        pnorm = jnp.sqrt(lax.optimization_barrier(jnp.sum(local * local, axis=2)) + 1e-08)
        return jnp.concatenate([att_values.transpose(1, 0, 2).reshape(RES_DEV, -1), local.transpose(1, 2, 0, 3).reshape(RES_DEV, -1), pnorm.transpose(1, 0, 2).reshape(RES_DEV, -1), att_pair.transpose(1, 0, 2).reshape(RES_DEV, -1)], axis=1).astype(jnp.bfloat16)
    features = lax.map(one_block, jnp.arange(N_BLK, dtype=jnp.int32) * 1).reshape(RES, -1)
    mixed = jnp.dot(features, w_out, preferred_element_type=jnp.float32) + single.astype(jnp.float32)
    center = mixed - lax.optimization_barrier(jnp.mean(mixed, axis=1, keepdims=True))
    snew = center * lax.rsqrt(lax.optimization_barrier(jnp.mean(center * center, axis=1, keepdims=True)) + 1e-05) * out_gain
    update = jnp.dot(snew, w_frame, precision=lax.Precision.HIGHEST)
    upd_rot = quat_rotation(update[:, 0], update[:, 1], update[:, 2])
    new_rot = jnp.einsum('xyn,yzn->xzn', rot, upd_rot, precision=lax.Precision.HIGHEST)
    new_trans = jnp.einsum('xyn,yn->xn', rot, update[:, 3:].T, precision=lax.Precision.HIGHEST) + trans
    frames_out = jnp.concatenate([new_rot.reshape(9, RES), new_trans], axis=0)
    return (snew.astype(jnp.bfloat16), frames_out)
```

```python
import math

import jax
import jax.numpy as jnp
import numpy as np
from jax import lax
from jax.experimental import pallas as pl
from jax.experimental.pallas import tpu as pltpu
from jax.sharding import PartitionSpec as P

F32 = jnp.float32
BF16 = jnp.bfloat16
HI = lax.Precision.HIGHEST

HEADS, HD, QP, VP, CZ, RANK, CS = 12, 16, 4, 8, 128, 64, 384
ROWS = 16
HPAD = 16
PACK = 512
C_HI, C_MID, C_LO, C_CHAIN, C_LIVE = 64, 76, 88, 100, 108
R_VAL, R_KP, R_VP, R_SEL, R_ALL = 192, 384, 528, 816, 832
K_P = (192, 336, 480)
K_ONE = 624
K_QSQ = 672
K_ALL = 768
C0 = math.sqrt(2.0 / math.pi)
GAMMA = (C0 * 0.044715) ** (1.0 / 3.0)
GB = C0 / GAMMA
S3 = math.sqrt(1.0 / 3.0)
COEF = math.sqrt(2.0 / (9.0 * QP)) / 2.0


def dot(a, b):
    return jnp.dot(a, b, preferred_element_type=F32)


def dot_nt(a, b):
    return lax.dot_general(a, b, (((1,), (1,)), ((), ())), preferred_element_type=F32)


def dot_hi(a, b):
    return jnp.dot(a, b, preferred_element_type=F32, precision=HI)


def split3(x):
    hi = x.astype(BF16).astype(F32)
    mid = (x - hi).astype(BF16).astype(F32)
    low = (x - hi - mid).astype(BF16).astype(F32)
    return hi, mid, low


def square_pad(x):
    r, c = x.shape
    if c < 128:
        x = jnp.concatenate([x, jnp.zeros((r, 128 - c), x.dtype)], axis=1)
    if r < 128:
        x = jnp.concatenate([x, jnp.zeros((128 - r, 128), x.dtype)], axis=0)
    return x


def pack_kernel(single_ref, angles_ref, trans_ref, right_ref, chain_ref, live_ref, out_ref, fr_ref, frt_ref):
    ang = angles_ref[...]
    cosines, sines = jnp.cos(ang), jnp.sin(ang)
    ca, cb, cc = cosines[0:1], cosines[1:2], cosines[2:3]
    sa, sb, sc = sines[0:1], sines[1:2], sines[2:3]
    rows = [
        ca * cb, -sa * cc + ca * sb * sc, sa * sc + ca * sb * cc,
        sa * cb, ca * cc + sa * sb * sc, -ca * sc + sa * sb * cc,
        -sb, cb * sc, cb * cc,
    ]
    tall = jnp.concatenate(
        rows
        + [trans_ref[...], chain_ref[...].astype(F32), live_ref[...].astype(F32), jnp.zeros((2, ROWS), F32)],
        axis=0,
    )
    frt_ref[...] = tall
    wide = square_pad(tall).T[0:ROWS]
    fr_ref[...] = wide
    lane = lax.broadcasted_iota(jnp.int32, (ROWS, 128), 1)
    frame = jnp.where(lane < 12, wide, 0.0)
    hi, mid, low = split3(frame)
    tile = pltpu.roll(hi, C_HI, 1) + pltpu.roll(mid, C_MID, 1) + pltpu.roll(low, C_LO, 1)
    chain = wide[:, 12:13]
    live = wide[:, 13:14]
    tile = tile + jnp.where((lane - C_CHAIN).astype(F32) == chain, jnp.where(lane >= C_CHAIN, 1.0, 0.0), 0.0)
    tile = tile + jnp.where(lane == C_LIVE, live, 0.0)
    right = jnp.concatenate([right_ref[...].astype(F32), jnp.zeros((ROWS, 64), F32)], axis=1)
    out_ref[:, 0:CS] = single_ref[...]
    out_ref[:, CS:PACK] = (tile + right).astype(BF16)


def query_kernel(
    single_ref, fr_ref, left_ref, chain_ref, wq_ref, wqp_ref, win_ref, cb_ref, wpo_ref, wb_ref, pw_ref,
    spread_ref, headsum_ref, mask_ref, a_ref, wall_ref, bd_ref, bdb_ref, q_scr,
):
    rows = single_ref[...]
    query = dot(rows, wq_ref[...]).astype(BF16).astype(F32)
    points = dot(rows, wqp_ref[...])
    fr = fr_ref[...]
    pts = [points[:, 48 * y : 48 * (y + 1)] for y in range(3)]
    coef = pw_ref[...] * COEF
    spread = dot_hi(coef, spread_ref[...])
    q_scr[:, 0:192] = query
    sq = jnp.zeros((ROWS, 48), F32)
    for x in range(3):
        g = fr[:, 9 + x : 10 + x]
        g = g + (fr[:, 3 * x : 3 * x + 1] * pts[0] + fr[:, 3 * x + 1 : 3 * x + 2] * pts[1] + fr[:, 3 * x + 2 : 3 * x + 3] * pts[2])
        sq = sq + g * g
        parts = split3(g * (8.0 * spread))
        for k in range(3):
            q_scr[:, K_P[k] + 48 * x : K_P[k] + 48 * (x + 1)] = parts[k]
    qsq = dot_hi(sq * (-4.0 * spread), headsum_ref[...])
    q_scr[:, K_ONE:K_QSQ] = jnp.ones((ROWS, 48), F32)
    parts = split3(qsq)
    for k in range(3):
        q_scr[:, K_QSQ + 16 * k : K_QSQ + 16 * (k + 1)] = parts[k]
    q_scr[:, K_QSQ + 48 : K_ALL] = jnp.zeros((ROWS, K_ALL - K_QSQ - 48), F32)
    mask = mask_ref[...]
    for i in range(ROWS):
        a_ref[i * HPAD : (i + 1) * HPAD, :] = (q_scr[i : i + 1, :] * mask).astype(BF16)
    left_t = square_pad(left_ref[...].astype(F32)).T
    win = win_ref[...].astype(F32) * GAMMA
    cb = cb_ref[...] * GAMMA
    row = lax.broadcasted_iota(jnp.int32, (64, 128), 0)
    for i in range(ROWS):
        w = left_t[0:64, i : i + 1] * win
        hi = w.astype(BF16)
        wall_ref[0:64, i * 128 : (i + 1) * 128] = hi
        wall_ref[128:192, i * 128 : (i + 1) * 128] = (w - hi.astype(F32)).astype(BF16)
        own = jnp.where(row - (C_CHAIN - 64) == chain_ref[i], jnp.broadcast_to(cb, (64, 128)), 0.0)
        own = jnp.where(row >= C_CHAIN - 64, own, 0.0)
        hi = own.astype(BF16)
        wall_ref[64:128, i * 128 : (i + 1) * 128] = hi
        wall_ref[192:256, i * 128 : (i + 1) * 128] = (own - hi.astype(F32)).astype(BF16)
    w = wpo_ref[...].astype(F32)
    w = (w - jnp.mean(w, axis=1, keepdims=True)) * (0.5 / GAMMA)
    bd_ref[...] = jnp.zeros((256, 256), BF16)
    bd_ref[0:128, 0:128] = w.astype(BF16)
    bd_ref[128:256, 128:256] = w.astype(BF16)
    wb = square_pad(wb_ref[...].astype(F32)).T[0:16].astype(BF16)
    bdb_ref[...] = jnp.zeros((32, 256), BF16)
    bdb_ref[0:16, 0:128] = wb
    bdb_ref[16:32, 128:256] = wb


def make_main(pieces, nblk, count):
    per_piece = 2048 // pieces
    blocks = 2048 // nblk

    def main_kernel(*refs):
        pk_hbm = refs[:pieces]
        (
            a_ref, wall_ref, bd_ref, bdb_ref, wt_ref, coef_ref, ksum_ref, bones_ref, vmask_ref,
            single_ref, fr_ref, frt_ref, wout_ref, gain_ref, wframe_ref,
            out_ref, frames_ref,
            pk, m_scr, l_scr, accp, accv, wbuf, l0, vt, bmat, apair, sems,
        ) = refs[pieces:]
        copies = [
            pltpu.make_async_copy(pk_hbm[i], pk.at[pl.ds(i * per_piece, per_piece)], sems.at[i])
            for i in range(pieces)
        ]
        for c in copies:
            c.start()
        m_scr[...] = jnp.full((256, 128), -1e30, F32)
        l_scr[...] = jnp.zeros((256, 128), F32)
        accp[...] = jnp.zeros((256, 256), F32)
        accv[...] = jnp.zeros((256, 512), F32)
        vt[480:512, :] = jnp.zeros((32, nblk), BF16)
        bmat[K_QSQ:K_ALL, :] = jnp.ones((K_ALL - K_QSQ, nblk), BF16)
        for c in copies:
            c.wait()

        def block(b, carry):
            rows = pk[pl.ds(pl.multiple_of(b * nblk, nblk), nblk), :]
            kvt = dot_nt(wt_ref[...], rows)
            bmat[0:192, :] = kvt[0:192].astype(BF16)
            vt[0:192, :] = kvt[R_VAL : R_VAL + 192].astype(BF16)
            sel = kvt[R_SEL : R_SEL + 16]
            ksq = None
            for x in range(3):
                r = [sel[3 * x + y : 3 * x + y + 1] for y in range(3)]
                t = sel[9 + x : 10 + x]
                kp = t
                vp = t
                for y in range(3):
                    kp = kp + r[y] * kvt[R_KP + 48 * y : R_KP + 48 * (y + 1)]
                    vp = vp + r[y] * kvt[R_VP + 96 * y : R_VP + 96 * (y + 1)]
                kb = kp.astype(BF16)
                for k in range(3):
                    bmat[K_P[k] + 48 * x : K_P[k] + 48 * (x + 1), :] = kb
                vt[192 + 96 * x : 192 + 96 * (x + 1), :] = vp.astype(BF16)
                kf = kb.astype(F32)
                ksq = kf * kf if ksq is None else ksq + kf * kf
            hi, mid, low = split3(ksq)
            both = jnp.concatenate([hi, mid, low], axis=0).astype(BF16)
            ks = dot(ksum_ref[...], both)
            dead = 100000.0 * (1.0 - sel[12:13])
            ks = ks * coef_ref[...] - (4.0 / S3) * dead
            hi, mid, low = split3(ks)
            bmat[K_ONE : K_ONE + 48, :] = jnp.concatenate([hi, mid, low], axis=0).astype(BF16)
            l0[...] = dot(a_ref[...], bmat[...]) * (S3 / 4.0)
            tile = rows[:, CS:PACK]
            wide = jnp.concatenate([tile, tile], axis=1)

            def pair(p, c2):
                r0 = pl.multiple_of(p * 32, 32)
                lane0 = pl.multiple_of(p * 256, 256)
                w = dot(wide, wall_ref[:, pl.ds(lane0, 256)])
                t = jnp.tanh(w * (w * w + GB))
                hid = (w + w * t).astype(BF16)
                center = dot(hid, bd_ref[...])
                cb = center.astype(BF16)
                sq = (center * center).astype(BF16)
                bias = dot_nt(bdb_ref[...], cb)
                var = dot_nt(bones_ref[...], sq)
                rs = lax.rsqrt(var + 1e-05)
                logits = l0[pl.ds(r0, 32), :] + bias * (rs * S3)
                top = m_scr[pl.ds(r0, 32), :]
                new = jnp.maximum(top, jnp.max(logits, axis=1, keepdims=True))
                factor = jnp.exp(top - new)
                m_scr[pl.ds(r0, 32), :] = new
                terms = jnp.exp(logits - new[:, 0:1])
                part = terms[:, 0:128]
                for k in range(1, nblk // 128):
                    part = part + terms[:, 128 * k : 128 * (k + 1)]
                l_scr[pl.ds(r0, 32), :] = l_scr[pl.ds(r0, 32), :] * factor + part
                wbuf[pl.ds(r0, 32), :] = terms.astype(BF16)
                wr = (terms * rs).astype(BF16)
                f2 = jnp.concatenate([factor, factor], axis=1)
                accp[pl.ds(r0, 32), :] = accp[pl.ds(r0, 32), :] * f2 + dot(wr, cb)
                f4 = jnp.concatenate([f2, f2], axis=1)
                accv[pl.ds(r0, 32), :] = accv[pl.ds(r0, 32), :] * f4
                return c2

            lax.fori_loop(0, 8, pair, 0, unroll=UNROLL)
            accv[...] += dot_nt(wbuf[...], vt[...])
            return carry

        lax.fori_loop(0, blocks, block, 0)

        inv = 1.0 / jnp.sum(l_scr[...], axis=1, keepdims=True)
        row = lax.broadcasted_iota(jnp.int32, (256, 128), 0)
        first = jnp.bitwise_and(row, 16) == 0
        for k in range(4):
            apair[...] = accv[:, 128 * k : 128 * (k + 1)] * inv
            total = None
            for h in range(HEADS):
                piece = apair[pl.ds(h, ROWS, stride=HPAD), :] * vmask_ref[h : h + 1, 128 * k : 128 * (k + 1)]
                total = piece if total is None else total + piece
            l0[0:ROWS, 128 * k : 128 * (k + 1)] = total
        apair[...] = jnp.where(first, accp[:, 0:128], accp[:, 128:256]) * inv
        attv = l0[0:ROWS, 0:512]
        mixed = single_ref[...].astype(F32)
        mixed = mixed + dot(attv[:, 0:192].astype(BF16), wout_ref[0:192, :])
        fr = fr_ref[...]
        rel = [attv[:, 192 + 96 * y : 192 + 96 * (y + 1)] - fr[:, 9 + y : 10 + y] for y in range(3)]
        norm = None
        for x in range(3):
            local = fr[:, x : x + 1] * rel[0] + fr[:, 3 + x : 4 + x] * rel[1] + fr[:, 6 + x : 7 + x] * rel[2]
            norm = local * local if norm is None else norm + local * local
            mixed = mixed + dot(local.astype(BF16), wout_ref[192 + 96 * x : 192 + 96 * (x + 1), :])
        norm = jnp.sqrt(norm + 1e-08)
        mixed = mixed + dot(norm.astype(BF16), wout_ref[480:576, :])
        for h in range(HEADS):
            mixed = mixed + dot(
                apair[pl.ds(h, ROWS, stride=HPAD), :].astype(BF16), wout_ref[576 + 128 * h : 576 + 128 * (h + 1), :]
            )
        mean = jnp.mean(mixed, axis=1, keepdims=True)
        center = mixed - mean
        snew = center * lax.rsqrt(jnp.mean(center * center, axis=1, keepdims=True) + 1e-05) * gain_ref[...]
        out_ref[...] = snew.astype(BF16)
        update = dot_hi(snew, wframe_ref[...])
        upd = square_pad(update).T
        ub, uc, ud = upd[0:1, 0:ROWS], upd[1:2, 0:ROWS], upd[2:3, 0:ROWS]
        n = jnp.sqrt(1.0 + ub * ub + uc * uc + ud * ud)
        ua = 1.0 / n
        ub, uc, ud = ub / n, uc / n, ud / n
        ru = [
            [ua * ua + ub * ub - uc * uc - ud * ud, 2.0 * (ub * uc - ua * ud), 2.0 * (ub * ud + ua * uc)],
            [2.0 * (ub * uc + ua * ud), ua * ua - ub * ub + uc * uc - ud * ud, 2.0 * (uc * ud - ua * ub)],
            [2.0 * (ub * ud - ua * uc), 2.0 * (uc * ud + ua * ub), ua * ua - ub * ub - uc * uc + ud * ud],
        ]
        frt = frt_ref[...]
        rot = [[frt[3 * x + y : 3 * x + y + 1] for y in range(3)] for x in range(3)]
        res = []
        for x in range(3):
            for z in range(3):
                res.append(rot[x][0] * ru[0][z] + rot[x][1] * ru[1][z] + rot[x][2] * ru[2][z])
        for x in range(3):
            s = frt[9 + x : 10 + x]
            for y in range(3):
                s = s + rot[x][y] * upd[3 + y : 4 + y, 0:ROWS]
            res.append(s)
        frames_ref[...] = jnp.concatenate(res, axis=0)

    return main_kernel


UNROLL = 2
NBLK = 512


def axis_perm(order_step, shift):
    strides = {"z": 32, "x": 8, "y": 2}
    perm = []
    for d in range(128):
        stride = strides[order_step[d % 2]]
        at = (d // stride) % 4
        perm.append((d, d + (((at + shift) % 4) - at) * stride))
    return perm


CORE = [(d, d ^ 1) for d in range(128)]
STAGES = (("y", "z"), ("x", "x"), ("z", "y"))


def per_device(
    single, angles, trans, left_factor, right_factor, chain, live,
    w_query, w_keyval, w_qpoints, w_kvpoints, w_pair_in, chain_bias, w_pair_out, w_bias,
    point_weight, w_out, out_gain, w_frame,
):
    vm = pl.BlockSpec(memory_space=pltpu.VMEM)
    sm = pl.BlockSpec(memory_space=pltpu.SMEM)
    anym = pl.BlockSpec(memory_space=pl.ANY)
    packed, fr, frt = pl.pallas_call(
        pack_kernel,
        out_shape=(
            jax.ShapeDtypeStruct((ROWS, PACK), BF16),
            jax.ShapeDtypeStruct((ROWS, 128), F32),
            jax.ShapeDtypeStruct((16, ROWS), F32),
        ),
        in_specs=[vm] * 6,
        out_specs=(vm, vm, vm),
    )(single, angles, trans, right_factor, chain[None], live[None])

    have = [packed]
    for stage in STAGES:
        block = have[0] if len(have) == 1 else jnp.concatenate(have, axis=0)
        have = [block] + [lax.ppermute(block, "blk", axis_perm(stage, s)) for s in (1, 2, 3)]
    pieces = have + [lax.ppermute(piece, "blk", CORE) for piece in have]

    head = np.arange(HPAD)
    mask = np.zeros((HPAD, K_ALL), np.float32)
    col = np.arange(192)
    mask[:, 0:192] = col[None] // HD == head[:, None]
    col = np.arange(144)
    for k in range(3):
        mask[:, K_P[k] : K_P[k] + 144] = (col[None] % 48) // QP == head[:, None]
    col = np.arange(96)
    mask[:, K_ONE : K_ONE + 96] = col[None] % 16 == head[:, None]
    mask[HEADS:] = 0.0
    col = np.arange(48)
    spread = (col[None] // QP == np.arange(HEADS)[:, None]).astype(np.float32)
    headsum = (col[:, None] // QP == head[None]).astype(np.float32)
    a_mat, wall, bd, bdb = pl.pallas_call(
        query_kernel,
        out_shape=(
            jax.ShapeDtypeStruct((256, K_ALL), BF16),
            jax.ShapeDtypeStruct((256, 2048), BF16),
            jax.ShapeDtypeStruct((256, 256), BF16),
            jax.ShapeDtypeStruct((32, 256), BF16),
        ),
        in_specs=[vm] * 3 + [sm] + [vm] * 10,
        out_specs=(vm,) * 4,
        scratch_shapes=[pltpu.VMEM((ROWS, K_ALL), F32)],
        compiler_params=pltpu.CompilerParams(vmem_limit_bytes=24 << 20),
        cost_estimate=pl.CostEstimate(flops=20_000_000, bytes_accessed=3_000_000, transcendentals=0),
    )(
        single, fr, left_factor, chain, w_query, w_qpoints, w_pair_in, chain_bias[None], w_pair_out, w_bias,
        point_weight[None], jnp.asarray(spread), jnp.asarray(headsum), jnp.asarray(mask),
    )

    kvp = w_kvpoints.reshape(CS, 3, HEADS, QP + VP)
    top = jnp.concatenate(
        [
            w_keyval,
            kvp[..., :QP].reshape(CS, 3 * HEADS * QP),
            kvp[..., QP:].reshape(CS, 3 * HEADS * VP),
        ],
        axis=1,
    ).T
    sel = np.zeros((16, PACK), np.float32)
    for v in range(12):
        for c in (C_HI, C_MID, C_LO):
            sel[v, CS + c + v] = 1.0
    sel[12, CS + C_LIVE] = 1.0
    wt = jnp.concatenate(
        [jnp.pad(top, ((0, 0), (0, PACK - CS))), jnp.asarray(sel, BF16)], axis=0
    )
    coef = jnp.pad(point_weight * (-4.0 * COEF), (0, HPAD - HEADS))[:, None]
    one = (np.arange(48)[None] // QP == head[:, None]).astype(np.float32)
    ksum = jnp.asarray(np.concatenate([one, one, one], axis=1), BF16)
    bones = np.zeros((32, 256), np.float32)
    bones[0:16, 0:128] = 1.0 / 128.0
    bones[16:32, 128:256] = 1.0 / 128.0
    vmask = np.zeros((HPAD, 512), np.float32)
    col = np.arange(192)
    vmask[:, 0:192] = col[None] // HD == head[:, None]
    col = np.arange(288)
    vmask[:, 192:480] = (col[None] % 96) // VP == head[:, None]
    vmask[HEADS:] = 0.0
    count = len(pieces)
    out, frames = pl.pallas_call(
        make_main(count, NBLK, count),
        out_shape=(
            jax.ShapeDtypeStruct((ROWS, CS), BF16),
            jax.ShapeDtypeStruct((12, ROWS), F32),
        ),
        in_specs=[anym] * count + [vm] * 15,
        out_specs=(vm, vm),
        scratch_shapes=[
            pltpu.VMEM((2048, PACK), BF16),
            pltpu.VMEM((256, 128), F32),
            pltpu.VMEM((256, 128), F32),
            pltpu.VMEM((256, 256), F32),
            pltpu.VMEM((256, 512), F32),
            pltpu.VMEM((256, NBLK), BF16),
            pltpu.VMEM((256, max(NBLK, 512)), F32),
            pltpu.VMEM((512, NBLK), BF16),
            pltpu.VMEM((K_ALL, NBLK), BF16),
            pltpu.VMEM((256, 128), F32),
            pltpu.SemaphoreType.DMA((count,)),
        ],
        compiler_params=pltpu.CompilerParams(vmem_limit_bytes=40 << 20),
        cost_estimate=pl.CostEstimate(flops=12_000_000_000, bytes_accessed=8_000_000, transcendentals=5_000_000),
    )(
        *pieces, a_mat, wall, bd, bdb, wt, coef, ksum, jnp.asarray(bones, BF16), jnp.asarray(vmask),
        single, fr, frt, w_out, out_gain[None], w_frame,
    )
    return out, frames


def solution(mesh):
    in_specs = (
        P("blk", None), P(None, "blk"), P(None, "blk"), P("blk", None), P("blk", None), P("blk"), P("blk"),
    ) + (P(),) * 12
    out_specs = (P("blk", None), P(None, "blk"))
    return jax.shard_map(per_device, mesh=mesh, in_specs=in_specs, out_specs=out_specs, check_vma=False)
```

```python
import math

import jax
import jax.numpy as jnp
from jax import lax
from jax.experimental import pallas as pl
from jax.experimental.pallas import tpu as pltpu
from jax.sharding import PartitionSpec as P

F32 = jnp.float32
BF16 = jnp.bfloat16
HI = lax.Precision.HIGHEST

HEADS, HD, QP, VP, CZ, RANK, CS = 12, 16, 4, 8, 128, 64, 384
ROWS = 16
HPAD = 16
PACK = 512
C_HI, C_MID, C_LO, C_CHAIN, C_LIVE = 64, 76, 88, 100, 108
R_VAL, R_KP, R_VP, R_SEL, R_TILE, R_ALL = 192, 384, 528, 816, 832, 960
K_P = (192, 336, 480)
K_ONE = 624
K_QSQ = 672
K_ALL = 768
C0 = math.sqrt(2.0 / math.pi)
GAMMA = (C0 * 0.044715) ** (1.0 / 3.0)
GB = C0 / GAMMA
S3 = math.sqrt(1.0 / 3.0)
PLANE = 16
PIECE = ROWS * PLANE
COEF = math.sqrt(2.0 / (9.0 * QP)) / 2.0


def dot(a, b):
    return jnp.dot(a, b, preferred_element_type=F32)


def dot_nt(a, b):
    return lax.dot_general(a, b, (((1,), (1,)), ((), ())), preferred_element_type=F32)


def dot_hi(a, b):
    return jnp.dot(a, b, preferred_element_type=F32, precision=HI)


def split3(x):
    hi = x.astype(BF16).astype(F32)
    mid = (x - hi).astype(BF16).astype(F32)
    low = (x - hi - mid).astype(BF16).astype(F32)
    return hi, mid, low


def square_pad(x):
    r, c = x.shape
    if c < 128:
        x = jnp.concatenate([x, jnp.zeros((r, 128 - c), x.dtype)], axis=1)
    if r < 128:
        x = jnp.concatenate([x, jnp.zeros((128 - r, 128), x.dtype)], axis=0)
    return x


def pack_kernel(single_ref, angles_ref, trans_ref, right_ref, chain_ref, live_ref, out_ref, fr_ref, frt_ref):
    ang = angles_ref[...]
    cosines, sines = jnp.cos(ang), jnp.sin(ang)
    ca, cb, cc = cosines[0:1], cosines[1:2], cosines[2:3]
    sa, sb, sc = sines[0:1], sines[1:2], sines[2:3]
    rows = [
        ca * cb, -sa * cc + ca * sb * sc, sa * sc + ca * sb * cc,
        sa * cb, ca * cc + sa * sb * sc, -ca * sc + sa * sb * cc,
        -sb, cb * sc, cb * cc,
    ]
    tall = jnp.concatenate(
        rows
        + [trans_ref[...], chain_ref[...].astype(F32), live_ref[...].astype(F32), jnp.zeros((2, ROWS), F32)],
        axis=0,
    )
    frt_ref[...] = tall
    wide = square_pad(tall).T[0:ROWS]
    fr_ref[...] = wide
    lane = lax.broadcasted_iota(jnp.int32, (ROWS, 128), 1)
    frame = jnp.where(lane < 12, wide, 0.0)
    hi, mid, low = split3(frame)
    tile = pltpu.roll(hi, C_HI, 1) + pltpu.roll(mid, C_MID, 1) + pltpu.roll(low, C_LO, 1)
    chain = wide[:, 12:13]
    live = wide[:, 13:14]
    tile = tile + jnp.where((lane - C_CHAIN).astype(F32) == chain, jnp.where(lane >= C_CHAIN, 1.0, 0.0), 0.0)
    tile = tile + jnp.where(lane == C_LIVE, live, 0.0)
    right = jnp.concatenate([right_ref[...].astype(F32), jnp.zeros((ROWS, 64), F32)], axis=1)
    row = single_ref[...]
    tile = (tile + right).astype(BF16)
    for k in range(PLANE):
        out_ref[ROWS * k : ROWS * (k + 1), 0:CS] = row
        out_ref[ROWS * k : ROWS * (k + 1), CS:PACK] = tile


def iota(shape, axis):
    return lax.broadcasted_iota(jnp.int32, shape, axis)


def modulo(x, m):
    return x - m * jnp.floor((x.astype(F32) + 0.5) * (1.0 / m)).astype(jnp.int32)


def one_where(condition):
    return jnp.where(condition, 1.0, 0.0)


def query_kernel(
    single_ref, fr_ref, left_ref, wq_ref, wqp_ref, win_ref, cb_ref, wpo_ref, wb_ref, pw_ref, wkv_ref, wkvp_ref,
    a_ref, wall_ref, cmat_ref, wt_ref, coef_ref, ksum_ref, q_scr,
):
    rows = single_ref[...]
    query = dot_nt(rows, wq_ref[...]).astype(BF16).astype(F32)
    points = dot_nt(rows, wqp_ref[...])
    fr = fr_ref[...]
    pts = [points[:, 48 * y : 48 * (y + 1)] for y in range(3)]
    coef = pw_ref[...] * COEF
    spread = dot_hi(coef, one_where(iota((HEADS, 48), 1) >> 2 == iota((HEADS, 48), 0)))
    q_scr[:, 0:192] = query
    sq = jnp.zeros((ROWS, 48), F32)
    for x in range(3):
        g = fr[:, 9 + x : 10 + x]
        g = g + (fr[:, 3 * x : 3 * x + 1] * pts[0] + fr[:, 3 * x + 1 : 3 * x + 2] * pts[1] + fr[:, 3 * x + 2 : 3 * x + 3] * pts[2])
        sq = sq + g * g
        parts = split3(g * (8.0 * spread))
        for k in range(3):
            q_scr[:, K_P[k] + 48 * x : K_P[k] + 48 * (x + 1)] = parts[k]
    qsq = dot_hi(sq * (-4.0 * spread), one_where(iota((48, HPAD), 0) >> 2 == iota((48, HPAD), 1)))
    q_scr[:, K_ONE:K_QSQ] = jnp.ones((ROWS, 48), F32)
    parts = split3(qsq)
    for k in range(3):
        q_scr[:, K_QSQ + 16 * k : K_QSQ + 16 * (k + 1)] = parts[k]
    q_scr[:, K_QSQ + 48 : K_ALL] = jnp.zeros((ROWS, K_ALL - K_QSQ - 48), F32)
    col, head = iota((HPAD, K_ALL), 1), iota((HPAD, K_ALL), 0)
    of_point = modulo(col, 48) >> 2
    own = jnp.where(col < 192, col >> 4, jnp.where(col < K_ONE, of_point, jnp.bitwise_and(col, 15)))
    mask = one_where((own == head) & (head < HEADS) & (col < K_QSQ + 48))
    for i in range(ROWS):
        a_ref[i * HPAD : (i + 1) * HPAD, :] = (q_scr[i : i + 1, :] * mask).astype(BF16)
    win_t = square_pad(win_ref[...].astype(F32)).T * GAMMA
    cb = cb_ref[...] * GAMMA
    cb_t = square_pad(cb).T[:, 0:1]
    lane = lax.broadcasted_iota(jnp.int32, (128, 128), 1).astype(F32)
    left = left_ref[...].astype(F32)
    left = jnp.concatenate([left, jnp.zeros((ROWS, 64), F32)], axis=1)
    for i in range(ROWS):
        w = win_t * left[i : i + 1, :]
        w = w + jnp.where(lane == fr[i : i + 1, 12:13] + C_CHAIN, cb_t, 0.0)
        hi = w.astype(BF16)
        wall_ref[i * 128 : (i + 1) * 128, 0:128] = hi
        wall_ref[i * 128 : (i + 1) * 128, 128:256] = (w - hi.astype(F32)).astype(BF16)
    w = wpo_ref[...].astype(F32)
    w = (w - jnp.mean(w, axis=1, keepdims=True)) * (0.5 / GAMMA)
    wb_t = jnp.concatenate([wb_ref[...].astype(F32), jnp.zeros((HPAD - HEADS, CZ), F32)], axis=0)
    w_t = w.T
    both = dot_hi(wb_t, w_t)
    hi = both.astype(BF16)
    low = (both - hi.astype(F32)).astype(BF16)
    cmat_ref[...] = jnp.zeros((320, 256), BF16)
    for k in range(2):
        lanes = slice(128 * k, 128 * (k + 1))
        cmat_ref[lanes, lanes] = w_t.astype(BF16)
        cmat_ref[256 + 16 * k : 272 + 16 * k, lanes] = hi
        cmat_ref[288 + 16 * k : 304 + 16 * k, lanes] = low
    wt_ref[0:384, 0:CS] = wkv_ref[...].astype(F32).T.astype(BF16)
    row = iota((432, 432), 0)
    is_key = row < 144
    val = row - 144
    axis = jnp.where(is_key, one_where(row >= 48) + one_where(row >= 96), one_where(val >= 96) + one_where(val >= 192))
    axis = axis.astype(jnp.int32)
    key_at, val_at = row - 48 * axis, val - 96 * axis
    source = jnp.where(
        is_key,
        (key_at >> 2) * (QP + VP) + jnp.bitwise_and(key_at, 3),
        (val_at >> 3) * (QP + VP) + QP + jnp.bitwise_and(val_at, 7),
    )
    perm = one_where(source + 144 * axis == iota((432, 432), 1)).astype(BF16)
    wt_ref[384:816, 0:CS] = dot(perm, wkvp_ref[...]).astype(BF16)
    wt_ref[0:R_ALL, CS:PACK] = jnp.zeros((R_ALL, PACK - CS), BF16)
    wt_ref[R_SEL:R_ALL, 0:CS] = jnp.zeros((R_ALL - R_SEL, CS), BF16)
    row, col = iota((16, 128), 0), iota((16, 128), 1)
    sel = (row < 12) & ((col - row == C_HI) | (col - row == C_MID) | (col - row == C_LO))
    sel = sel | ((row == 12) & (col == C_LIVE))
    wt_ref[R_SEL:R_TILE, CS:PACK] = one_where(sel).astype(BF16)
    wt_ref[R_TILE:R_ALL, CS:PACK] = one_where(iota((128, 128), 0) == iota((128, 128), 1)).astype(BF16)
    ksum_ref[...] = one_where(modulo(iota((HPAD, 144), 1), 48) >> 2 == iota((HPAD, 144), 0)).astype(BF16)
    sub = lax.broadcasted_iota(jnp.int32, (16, HEADS), 0)
    col = lax.broadcasted_iota(jnp.int32, (16, HEADS), 1)
    coef_ref[...] = jnp.broadcast_to(
        jnp.sum(jnp.where(sub == col, -4.0 * coef, 0.0), axis=1, keepdims=True), (16, 128)
    )


def attend(pieces, ops, state_in, state_out, scr):
    a_ref, wall_ref, cmat_ref, wt_ref, coef_ref, ksum_ref = ops
    m_out, l_out, accp, accv = state_out
    wbuf, l0, vt, bmat, wide, cbuf, rsbuf = scr
    n = PIECE * len(pieces)
    vt[480:512, :] = jnp.zeros((32, n), BF16)
    bmat[K_QSQ:K_ALL, :] = jnp.ones((K_ALL - K_QSQ, n), BF16)
    coef = coef_ref[:, 0:1]
    for i, piece in enumerate(pieces):
        at = slice(PIECE * i, PIECE * (i + 1))
        kvt = dot_nt(wt_ref[...], piece[...])
        tile = kvt[R_TILE : R_TILE + 128].astype(BF16)
        wide[0:128, at] = tile
        wide[128:256, at] = tile
        bmat[0:192, at] = kvt[0:192].astype(BF16)
        vt[0:192, at] = kvt[R_VAL : R_VAL + 192].astype(BF16)
        sel = kvt[R_SEL : R_SEL + 16]
        ksq = None
        for x in range(3):
            r = [sel[3 * x + y : 3 * x + y + 1] for y in range(3)]
            t = sel[9 + x : 10 + x]
            kp = t
            vp = t
            for y in range(3):
                kp = kp + r[y] * kvt[R_KP + 48 * y : R_KP + 48 * (y + 1)]
                vp = vp + r[y] * kvt[R_VP + 96 * y : R_VP + 96 * (y + 1)]
            kb = kp.astype(BF16)
            for k in range(3):
                bmat[K_P[k] + 48 * x : K_P[k] + 48 * (x + 1), at] = kb
            vt[192 + 96 * x : 192 + 96 * (x + 1), at] = vp.astype(BF16)
            kf = kb.astype(F32)
            ksq = kf * kf if ksq is None else ksq + kf * kf
        hi, mid, low = split3(ksq)
        ks = dot(ksum_ref[...], jnp.concatenate([hi, mid, low], axis=0).astype(BF16))
        dead = 100000.0 * (1.0 - sel[12:13])
        ks = ks * coef - (4.0 / S3) * dead
        hi, mid, low = split3(ks)
        bmat[K_ONE : K_ONE + 48, at] = jnp.concatenate([hi, mid, low], axis=0).astype(BF16)
    l0[...] = dot(a_ref[...], bmat[...]) * (S3 / 4.0)

    def pair(p, carry):
        r0 = pl.multiple_of(p * 32, 32)
        w = dot(wall_ref[pl.ds(pl.multiple_of(p * 256, 256), 256), :], wide[...])
        t = jnp.tanh(w * (w * w + GB))
        hid = (w + w * t).astype(BF16)
        full = dot(cmat_ref[...], hid)
        center = full[0:256]
        cbuf[p] = center.astype(BF16)
        sq = center * center
        rs = []
        for k in range(2):
            var = jnp.sum(sq[128 * k : 128 * (k + 1)], axis=0, keepdims=True) * (1.0 / CZ)
            rs.append(jnp.broadcast_to(lax.rsqrt(var + 1e-05), (16, n)))
        rs = jnp.concatenate(rs, axis=0)
        l0[pl.ds(r0, 32), :] = l0[pl.ds(r0, 32), :] + (full[256:288] + full[288:320]) * (rs * S3)
        rsbuf[pl.ds(r0, 32), :] = rs
        return carry

    lax.fori_loop(0, 8, pair, 0, unroll=UNROLL_PAIR)

    def soft(p, carry):
        r0 = pl.multiple_of(p * 32, 32)
        at = pl.ds(r0, 32)
        logits = l0[at, :]
        rs = rsbuf[at, :]
        new = jnp.max(logits, axis=1, keepdims=True)
        if state_in is not None:
            top = state_in[0][at, :]
            new = jnp.maximum(top, new)
            factor = jnp.exp(top - new)
        terms = jnp.exp(logits - new[:, 0:1])
        m_out[at, :] = jnp.broadcast_to(new, (32, 128))
        part = terms[:, 0:128]
        for k in range(1, n // 128):
            part = part + terms[:, 128 * k : 128 * (k + 1)]
        wbuf[at, :] = terms.astype(BF16)
        pair_sum = dot_nt((terms * rs).astype(BF16), cbuf[p])
        if state_in is not None:
            part = part + state_in[1][at, :] * factor
            f2 = jnp.concatenate([factor, factor], axis=1)
            pair_sum = pair_sum + state_in[2][at, :] * f2
            accv[at, :] = state_in[3][at, :] * jnp.concatenate([f2, f2], axis=1)
        l_out[at, :] = part
        accp[at, :] = pair_sum
        return carry

    lax.fori_loop(0, 8, soft, 0, unroll=UNROLL_SOFT)
    sums = dot_nt(wbuf[...], vt[...])
    accv[...] = sums if state_in is None else accv[...] + sums


def make_first(count):
    def first_kernel(*refs):
        attend(refs[:count], refs[count : count + 6], None, refs[count + 6 : count + 10], refs[count + 10 :])

    return first_kernel


def make_next(count):
    def next_kernel(*refs):
        attend(refs[:count], refs[count : count + 6], refs[count + 6 : count + 10], refs[count + 10 : count + 14], refs[count + 14 :])

    return next_kernel


def attend_cost(count):
    return pl.CostEstimate(flops=3_000_000_000 * count, bytes_accessed=4_000_000, transcendentals=600_000 * count)


def make_last(count):
    def last_kernel(*refs):
        ops = refs[count : count + 6]
        state_in = refs[count + 6 : count + 10]
        single_ref, fr_ref, frt_ref, wout_ref, gain_ref, wframe_ref, out_ref, frames_ref = refs[
            count + 10 : count + 18
        ]
        m_scr, l_scr, accp, accv, apair = refs[count + 18 : count + 23]
        scr = refs[count + 23 :]
        l0 = scr[1]
        attend(refs[:count], ops, state_in, (m_scr, l_scr, accp, accv), scr)
        inv = 1.0 / jnp.sum(l_scr[...], axis=1, keepdims=True)
        row = lax.broadcasted_iota(jnp.int32, (256, 128), 0)
        first = jnp.bitwise_and(row, 16) == 0
        col, head = iota((HPAD, 512), 1), iota((HPAD, 512), 0)
        own = jnp.where(col < 192, col >> 4, modulo(col, 96) >> 3)
        vmask = one_where((own == head) & (col < 480))
        for k in range(4):
            apair[...] = accv[:, 128 * k : 128 * (k + 1)] * inv
            total = None
            for h in range(HEADS):
                piece = apair[pl.ds(h, ROWS, stride=HPAD), :] * vmask[h : h + 1, 128 * k : 128 * (k + 1)]
                total = piece if total is None else total + piece
            l0[0:ROWS, 128 * k : 128 * (k + 1)] = total
        apair[...] = jnp.where(first, accp[:, 0:128], accp[:, 128:256]) * inv
        attv = l0[0:ROWS, 0:512]
        mixed = single_ref[...].astype(F32)
        mixed = mixed + dot(attv[:, 0:192].astype(BF16), wout_ref[0:192, :])
        fr = fr_ref[...]
        rel = [attv[:, 192 + 96 * y : 192 + 96 * (y + 1)] - fr[:, 9 + y : 10 + y] for y in range(3)]
        norm = None
        for x in range(3):
            local = fr[:, x : x + 1] * rel[0] + fr[:, 3 + x : 4 + x] * rel[1] + fr[:, 6 + x : 7 + x] * rel[2]
            norm = local * local if norm is None else norm + local * local
            mixed = mixed + dot(local.astype(BF16), wout_ref[192 + 96 * x : 192 + 96 * (x + 1), :])
        norm = jnp.sqrt(norm + 1e-08)
        mixed = mixed + dot(norm.astype(BF16), wout_ref[480:576, :])
        for h in range(HEADS):
            mixed = mixed + dot(
                apair[pl.ds(h, ROWS, stride=HPAD), :].astype(BF16), wout_ref[576 + 128 * h : 576 + 128 * (h + 1), :]
            )
        mean = jnp.mean(mixed, axis=1, keepdims=True)
        center = mixed - mean
        snew = center * lax.rsqrt(jnp.mean(center * center, axis=1, keepdims=True) + 1e-05) * gain_ref[...].reshape(1, CS)
        out_ref[...] = snew.astype(BF16)
        upd = lax.dot_general(
            wframe_ref[...], snew, (((1,), (1,)), ((), ())), preferred_element_type=F32, precision=HI
        )
        ub, uc, ud = upd[0:1, 0:ROWS], upd[1:2, 0:ROWS], upd[2:3, 0:ROWS]
        n = jnp.sqrt(1.0 + ub * ub + uc * uc + ud * ud)
        ua = 1.0 / n
        ub, uc, ud = ub / n, uc / n, ud / n
        ru = [
            [ua * ua + ub * ub - uc * uc - ud * ud, 2.0 * (ub * uc - ua * ud), 2.0 * (ub * ud + ua * uc)],
            [2.0 * (ub * uc + ua * ud), ua * ua - ub * ub + uc * uc - ud * ud, 2.0 * (uc * ud - ua * ub)],
            [2.0 * (ub * ud - ua * uc), 2.0 * (uc * ud + ua * ub), ua * ua - ub * ub - uc * uc + ud * ud],
        ]
        frt = frt_ref[...]
        rot = [[frt[3 * x + y : 3 * x + y + 1] for y in range(3)] for x in range(3)]
        res = []
        for x in range(3):
            for z in range(3):
                res.append(rot[x][0] * ru[0][z] + rot[x][1] * ru[1][z] + rot[x][2] * ru[2][z])
        for x in range(3):
            s = frt[9 + x : 10 + x]
            for y in range(3):
                s = s + rot[x][y] * upd[3 + y : 4 + y, 0:ROWS]
            res.append(s)
        frames_ref[...] = jnp.concatenate(res, axis=0)

    return last_kernel


UNROLL_PAIR = 8
UNROLL_SOFT = 8


STRIDE = {"z": 32, "x": 8, "y": 2}
FIRST = (("x", "y"), ("x", "z"))
SECOND = ("z", "y")


def plane_groups():
    groups = {}
    for d in range(128):
        key = d
        for axis in FIRST[d % 2]:
            key -= ((d // STRIDE[axis]) % 4) * STRIDE[axis]
        groups.setdefault(key, []).append(d)
    return list(groups.values())


def axis_perm(shift):
    perm = []
    for d in range(128):
        stride = STRIDE[SECOND[d % 2]]
        at = (d // stride) % 4
        perm.append((d, d + (((at + shift) % 4) - at) * stride))
    return perm


STATE = ((256, 128), (256, 128), (256, 256), (256, 512))
CORE = [(d, d ^ 1) for d in range(128)]


def attend_scratch(n):
    return [
        pltpu.VMEM((256, n), BF16),
        pltpu.VMEM((256, n), F32),
        pltpu.VMEM((512, n), BF16),
        pltpu.VMEM((K_ALL, n), BF16),
        pltpu.VMEM((256, n), BF16),
        pltpu.VMEM((8, 256, n), BF16),
        pltpu.VMEM((256, n), F32),
    ]


def per_device(
    single, angles, trans, left_factor, right_factor, chain, live,
    w_query, w_keyval, w_qpoints, w_kvpoints, w_pair_in, chain_bias, w_pair_out, w_bias,
    point_weight, w_out, out_gain, w_frame,
):
    vm = pl.BlockSpec(memory_space=pltpu.VMEM)
    packed, fr, frt = pl.pallas_call(
        pack_kernel,
        out_shape=(
            jax.ShapeDtypeStruct((PIECE, PACK), BF16),
            jax.ShapeDtypeStruct((ROWS, 128), F32),
            jax.ShapeDtypeStruct((16, ROWS), F32),
        ),
        in_specs=[vm] * 6,
        out_specs=(vm, vm, vm),
        cost_estimate=pl.CostEstimate(flops=4_000_000_000, bytes_accessed=8_000_000, transcendentals=1000),
    )(single, angles, trans, right_factor, chain[None], live[None])

    own = lax.all_to_all(packed, "blk", 0, 0, tiled=True, axis_index_groups=plane_groups())
    near = [own, lax.ppermute(own, "blk", CORE)]
    far = [lax.ppermute(own, "blk", axis_perm(s)) for s in (1, 3, 2)]

    near[1], single_q = lax.optimization_barrier((near[1], single))
    ops = pl.pallas_call(
        query_kernel,
        out_shape=(
            jax.ShapeDtypeStruct((256, K_ALL), BF16),
            jax.ShapeDtypeStruct((2048, 256), BF16),
            jax.ShapeDtypeStruct((320, 256), BF16),
            jax.ShapeDtypeStruct((R_ALL, PACK), BF16),
            jax.ShapeDtypeStruct((16, 128), F32),
            jax.ShapeDtypeStruct((HPAD, 144), BF16),
        ),
        in_specs=[vm] * 12,
        out_specs=(vm,) * 6,
        scratch_shapes=[pltpu.VMEM((ROWS, K_ALL), F32)],
        compiler_params=pltpu.CompilerParams(vmem_limit_bytes=16 << 20),
        cost_estimate=pl.CostEstimate(flops=600_000_000, bytes_accessed=5_000_000, transcendentals=0),
    )(
        single_q, fr, left_factor, w_query.T, w_qpoints.T, w_pair_in, chain_bias[None], w_pair_out, w_bias.T,
        point_weight[None], w_keyval, w_kvpoints.T,
    )
    scratch = [pltpu.VMEM(shape, F32) for shape in STATE]
    state = pl.pallas_call(
        make_first(len(near)),
        out_shape=tuple(jax.ShapeDtypeStruct(shape, F32) for shape in STATE),
        in_specs=[vm] * (len(near) + len(ops)),
        out_specs=(vm,) * 4,
        scratch_shapes=attend_scratch(PIECE * len(near)),
        compiler_params=pltpu.CompilerParams(vmem_limit_bytes=12 << 20),
        cost_estimate=attend_cost(len(near)),
    )(*near, *ops)
    far, state = lax.optimization_barrier((far, state))
    other = [lax.ppermute(piece, "blk", CORE) for piece in far]
    state = pl.pallas_call(
        make_next(len(far)),
        out_shape=tuple(jax.ShapeDtypeStruct(shape, F32) for shape in STATE),
        in_specs=[vm] * (len(far) + len(ops) + 4),
        out_specs=(vm,) * 4,
        scratch_shapes=attend_scratch(PIECE * len(far)),
        compiler_params=pltpu.CompilerParams(vmem_limit_bytes=20 << 20),
        cost_estimate=attend_cost(len(far)),
    )(*far, *ops, *state)
    out, frames = pl.pallas_call(
        make_last(len(other)),
        out_shape=(
            jax.ShapeDtypeStruct((ROWS, CS), BF16),
            jax.ShapeDtypeStruct((12, ROWS), F32),
        ),
        in_specs=[vm] * (len(other) + len(ops) + 4 + 6),
        out_specs=(vm, vm),
        scratch_shapes=scratch + [pltpu.VMEM((256, 128), F32)] + attend_scratch(PIECE * len(other)),
        compiler_params=pltpu.CompilerParams(vmem_limit_bytes=20 << 20),
        cost_estimate=attend_cost(len(other)),
    )(*other, *ops, *state, single, fr, frt, w_out, out_gain, w_frame.T)
    return out, frames


def solution(mesh):
    in_specs = (
        P("blk", None), P(None, "blk"), P(None, "blk"), P("blk", None), P("blk", None), P("blk"), P("blk"),
    ) + (P(),) * 12
    out_specs = (P("blk", None), P(None, "blk"))
    return jax.shard_map(per_device, mesh=mesh, in_specs=in_specs, out_specs=out_specs, check_vma=False)
```

```python
import math

import jax
import jax.numpy as jnp
from jax import lax
from jax.experimental import pallas as pl
from jax.experimental.pallas import tpu as pltpu
from jax.sharding import PartitionSpec as P

F32 = jnp.float32
BF16 = jnp.bfloat16
HI = lax.Precision.HIGHEST

HEADS, HD, QP, VP, CZ, RANK, CS = 12, 16, 4, 8, 128, 64, 384
ROWS = 16
HPAD = 16
PACK = 512
C_HI, C_MID, C_LO, C_CHAIN, C_LIVE = 64, 76, 88, 100, 108
R_VAL, R_KP, R_VP, R_SEL, R_TILE, R_ALL = 192, 384, 528, 816, 832, 960
K_P = (192, 336, 480)
K_ONE = 624
K_QSQ = 672
K_ALL = 768
C0 = math.sqrt(2.0 / math.pi)
GAMMA = (C0 * 0.044715) ** (1.0 / 3.0)
GB = C0 / GAMMA
S3 = math.sqrt(1.0 / 3.0)
PLANE = 16
PIECE = ROWS * PLANE
COEF = math.sqrt(2.0 / (9.0 * QP)) / 2.0


def dot(a, b):
    return jnp.dot(a, b, preferred_element_type=F32)


def dot_nt(a, b):
    return lax.dot_general(a, b, (((1,), (1,)), ((), ())), preferred_element_type=F32)


def dot_hi(a, b):
    return jnp.dot(a, b, preferred_element_type=F32, precision=HI)


def split3(x):
    hi = x.astype(BF16).astype(F32)
    mid = (x - hi).astype(BF16).astype(F32)
    low = (x - hi - mid).astype(BF16).astype(F32)
    return hi, mid, low


def square_pad(x):
    r, c = x.shape
    if c < 128:
        x = jnp.concatenate([x, jnp.zeros((r, 128 - c), x.dtype)], axis=1)
    if r < 128:
        x = jnp.concatenate([x, jnp.zeros((128 - r, 128), x.dtype)], axis=0)
    return x


def pack_kernel(single_ref, angles_ref, trans_ref, right_ref, chain_ref, live_ref, out_ref, fr_ref, frt_ref):
    ang = angles_ref[...]
    cosines, sines = jnp.cos(ang), jnp.sin(ang)
    ca, cb, cc = cosines[0:1], cosines[1:2], cosines[2:3]
    sa, sb, sc = sines[0:1], sines[1:2], sines[2:3]
    rows = [
        ca * cb, -sa * cc + ca * sb * sc, sa * sc + ca * sb * cc,
        sa * cb, ca * cc + sa * sb * sc, -ca * sc + sa * sb * cc,
        -sb, cb * sc, cb * cc,
    ]
    tall = jnp.concatenate(
        rows
        + [trans_ref[...], chain_ref[...].astype(F32), live_ref[...].astype(F32), jnp.zeros((2, ROWS), F32)],
        axis=0,
    )
    frt_ref[...] = tall
    wide = square_pad(tall).T[0:ROWS]
    fr_ref[...] = wide
    lane = lax.broadcasted_iota(jnp.int32, (ROWS, 128), 1)
    frame = jnp.where(lane < 12, wide, 0.0)
    hi, mid, low = split3(frame)
    tile = pltpu.roll(hi, C_HI, 1) + pltpu.roll(mid, C_MID, 1) + pltpu.roll(low, C_LO, 1)
    chain = wide[:, 12:13]
    live = wide[:, 13:14]
    tile = tile + jnp.where((lane - C_CHAIN).astype(F32) == chain, jnp.where(lane >= C_CHAIN, 1.0, 0.0), 0.0)
    tile = tile + jnp.where(lane == C_LIVE, live, 0.0)
    right = jnp.concatenate([right_ref[...].astype(F32), jnp.zeros((ROWS, 64), F32)], axis=1)
    row = single_ref[...]
    tile = (tile + right).astype(BF16)
    for k in range(PLANE):
        out_ref[ROWS * k : ROWS * (k + 1), 0:CS] = row
        out_ref[ROWS * k : ROWS * (k + 1), CS:PACK] = tile


def iota(shape, axis):
    return lax.broadcasted_iota(jnp.int32, shape, axis)


def modulo(x, m):
    return x - m * jnp.floor((x.astype(F32) + 0.5) * (1.0 / m)).astype(jnp.int32)


def one_where(condition):
    return jnp.where(condition, 1.0, 0.0)


def query_kernel(
    single_ref, fr_ref, left_ref, wq_ref, wqp_ref, win_ref, cb_ref, wpo_ref, wb_ref, pw_ref, wkv_ref, wkvp_ref,
    a_ref, wall_ref, cmat_ref, wt_ref, coef_ref, ksum_ref, q_scr,
):
    rows = single_ref[...]
    query = dot_nt(rows, wq_ref[...]).astype(BF16).astype(F32)
    points = dot_nt(rows, wqp_ref[...])
    fr = fr_ref[...]
    pts = [points[:, 48 * y : 48 * (y + 1)] for y in range(3)]
    coef = pw_ref[...] * COEF
    spread = dot_hi(coef, one_where(iota((HEADS, 48), 1) >> 2 == iota((HEADS, 48), 0)))
    q_scr[:, 0:192] = query
    sq = jnp.zeros((ROWS, 48), F32)
    for x in range(3):
        g = fr[:, 9 + x : 10 + x]
        g = g + (fr[:, 3 * x : 3 * x + 1] * pts[0] + fr[:, 3 * x + 1 : 3 * x + 2] * pts[1] + fr[:, 3 * x + 2 : 3 * x + 3] * pts[2])
        sq = sq + g * g
        parts = split3(g * (8.0 * spread))
        for k in range(3):
            q_scr[:, K_P[k] + 48 * x : K_P[k] + 48 * (x + 1)] = parts[k]
    qsq = dot_hi(sq * (-4.0 * spread), one_where(iota((48, HPAD), 0) >> 2 == iota((48, HPAD), 1)))
    q_scr[:, K_ONE:K_QSQ] = jnp.ones((ROWS, 48), F32)
    parts = split3(qsq)
    for k in range(3):
        q_scr[:, K_QSQ + 16 * k : K_QSQ + 16 * (k + 1)] = parts[k]
    q_scr[:, K_QSQ + 48 : K_ALL] = jnp.zeros((ROWS, K_ALL - K_QSQ - 48), F32)
    col, head = iota((HPAD, K_ALL), 1), iota((HPAD, K_ALL), 0)
    of_point = modulo(col, 48) >> 2
    own = jnp.where(col < 192, col >> 4, jnp.where(col < K_ONE, of_point, jnp.bitwise_and(col, 15)))
    mask = one_where((own == head) & (head < HEADS) & (col < K_QSQ + 48))
    for i in range(ROWS):
        a_ref[i * HPAD : (i + 1) * HPAD, :] = (q_scr[i : i + 1, :] * mask).astype(BF16)
    win_t = square_pad(win_ref[...].astype(F32)).T * GAMMA
    cb = cb_ref[...] * GAMMA
    cb_t = square_pad(cb).T[:, 0:1]
    lane = lax.broadcasted_iota(jnp.int32, (128, 128), 1).astype(F32)
    left = left_ref[...].astype(F32)
    left = jnp.concatenate([left, jnp.zeros((ROWS, 64), F32)], axis=1)
    for i in range(ROWS):
        w = win_t * left[i : i + 1, :]
        w = w + jnp.where(lane == fr[i : i + 1, 12:13] + C_CHAIN, cb_t, 0.0)
        hi = w.astype(BF16)
        wall_ref[i * 128 : (i + 1) * 128, 0:128] = hi
        wall_ref[i * 128 : (i + 1) * 128, 128:256] = (w - hi.astype(F32)).astype(BF16)
    w = wpo_ref[...].astype(F32)
    w = (w - jnp.mean(w, axis=1, keepdims=True)) * (0.5 / GAMMA)
    wb_t = jnp.concatenate([wb_ref[...].astype(F32), jnp.zeros((HPAD - HEADS, CZ), F32)], axis=0)
    w_t = w.T
    both = dot_hi(wb_t, w_t)
    hi = both.astype(BF16)
    low = (both - hi.astype(F32)).astype(BF16)
    cmat_ref[...] = jnp.zeros((320, 256), BF16)
    for k in range(2):
        lanes = slice(128 * k, 128 * (k + 1))
        cmat_ref[lanes, lanes] = w_t.astype(BF16)
        cmat_ref[256 + 16 * k : 272 + 16 * k, lanes] = hi
        cmat_ref[288 + 16 * k : 304 + 16 * k, lanes] = low
    wt_ref[0:384, 0:CS] = wkv_ref[...].astype(F32).T.astype(BF16)
    row = iota((432, 432), 0)
    is_key = row < 144
    val = row - 144
    axis = jnp.where(is_key, one_where(row >= 48) + one_where(row >= 96), one_where(val >= 96) + one_where(val >= 192))
    axis = axis.astype(jnp.int32)
    key_at, val_at = row - 48 * axis, val - 96 * axis
    source = jnp.where(
        is_key,
        (key_at >> 2) * (QP + VP) + jnp.bitwise_and(key_at, 3),
        (val_at >> 3) * (QP + VP) + QP + jnp.bitwise_and(val_at, 7),
    )
    perm = one_where(source + 144 * axis == iota((432, 432), 1)).astype(BF16)
    wt_ref[384:816, 0:CS] = dot(perm, wkvp_ref[...]).astype(BF16)
    wt_ref[0:R_ALL, CS:PACK] = jnp.zeros((R_ALL, PACK - CS), BF16)
    wt_ref[R_SEL:R_ALL, 0:CS] = jnp.zeros((R_ALL - R_SEL, CS), BF16)
    row, col = iota((16, 128), 0), iota((16, 128), 1)
    sel = (row < 12) & ((col - row == C_HI) | (col - row == C_MID) | (col - row == C_LO))
    sel = sel | ((row == 12) & (col == C_LIVE))
    wt_ref[R_SEL:R_TILE, CS:PACK] = one_where(sel).astype(BF16)
    wt_ref[R_TILE:R_ALL, CS:PACK] = one_where(iota((128, 128), 0) == iota((128, 128), 1)).astype(BF16)
    ksum_ref[...] = one_where(modulo(iota((HPAD, 144), 1), 48) >> 2 == iota((HPAD, 144), 0)).astype(BF16)
    sub = lax.broadcasted_iota(jnp.int32, (16, HEADS), 0)
    col = lax.broadcasted_iota(jnp.int32, (16, HEADS), 1)
    coef_ref[...] = jnp.broadcast_to(
        jnp.sum(jnp.where(sub == col, -4.0 * coef, 0.0), axis=1, keepdims=True), (16, 128)
    )


def attend(pieces, ops, state_in, state_out, scr):
    a_ref, wall_ref, cmat_ref, wt_ref, coef_ref, ksum_ref = ops
    m_out, l_out, accp, accv = state_out
    wbuf, l0, vt, bmat, wide, cbuf, rsbuf = scr
    n = PIECE * len(pieces)
    vt[480:512, :] = jnp.zeros((32, n), BF16)
    bmat[K_QSQ:K_ALL, :] = jnp.ones((K_ALL - K_QSQ, n), BF16)
    coef = coef_ref[:, 0:1]
    rows = jnp.concatenate([piece[...] for piece in pieces], axis=0)
    for at in (slice(0, n),):
        kvt = dot_nt(wt_ref[0:R_SEL, 0:CS], rows[:, 0:CS])
        low = dot_nt(wt_ref[R_SEL:R_ALL, CS:PACK], rows[:, CS:PACK])
        tile = low[R_TILE - R_SEL :].astype(BF16)
        wide[0:128, at] = tile
        wide[128:256, at] = tile
        bmat[0:192, at] = kvt[0:192].astype(BF16)
        vt[0:192, at] = kvt[R_VAL : R_VAL + 192].astype(BF16)
        sel = low[0:16]
        ksq = None
        for x in range(3):
            r = [sel[3 * x + y : 3 * x + y + 1] for y in range(3)]
            t = sel[9 + x : 10 + x]
            kp = t
            vp = t
            for y in range(3):
                kp = kp + r[y] * kvt[R_KP + 48 * y : R_KP + 48 * (y + 1)]
                vp = vp + r[y] * kvt[R_VP + 96 * y : R_VP + 96 * (y + 1)]
            kb = kp.astype(BF16)
            for k in range(3):
                bmat[K_P[k] + 48 * x : K_P[k] + 48 * (x + 1), at] = kb
            vt[192 + 96 * x : 192 + 96 * (x + 1), at] = vp.astype(BF16)
            kf = kb.astype(F32)
            ksq = kf * kf if ksq is None else ksq + kf * kf
        hi, mid, lo = split3(ksq)
        ks = dot(ksum_ref[...], jnp.concatenate([hi, mid, lo], axis=0).astype(BF16))
        dead = 100000.0 * (1.0 - sel[12:13])
        ks = ks * coef - (4.0 / S3) * dead
        hi, mid, lo = split3(ks)
        bmat[K_ONE : K_ONE + 48, at] = jnp.concatenate([hi, mid, lo], axis=0).astype(BF16)
    l0[...] = dot(a_ref[...], bmat[...]) * (S3 / 4.0)

    def stage1(p):
        return dot(wall_ref[p * 256 : (p + 1) * 256, :], wide[...])

    def stage2(w):
        t = jnp.tanh(w * (w * w + GB))
        hid = (w + w * t).astype(BF16)
        return dot(cmat_ref[...], hid)

    def stage3(p, full):
        at = slice(p * 32, (p + 1) * 32)
        center = full[0:256]
        cb = center.astype(BF16)
        sq = center * center
        rs = []
        for k in range(2):
            var = jnp.sum(sq[128 * k : 128 * (k + 1)], axis=0, keepdims=True) * (1.0 / CZ)
            rs.append(jnp.broadcast_to(lax.rsqrt(var + 1e-05), (16, n)))
        rs = jnp.concatenate(rs, axis=0)
        logits = l0[at, :] + (full[256:288] + full[288:320]) * (rs * S3)
        new = jnp.max(logits, axis=1, keepdims=True)
        factor = None
        if state_in is not None:
            top = state_in[0][at, :]
            new = jnp.maximum(top, new)
            factor = jnp.exp(top - new)
        terms = jnp.exp(logits - new[:, 0:1])
        m_out[at, :] = jnp.broadcast_to(new, (32, 128))
        part = terms[:, 0:128]
        for k in range(1, n // 128):
            part = part + terms[:, 128 * k : 128 * (k + 1)]
        wbuf[at, :] = terms.astype(BF16)
        return cb, (terms * rs).astype(BF16), part, factor

    def stage4(p, cb, wr, part, factor):
        at = slice(p * 32, (p + 1) * 32)
        pair_sum = dot_nt(wr, cb)
        if state_in is not None:
            part = part + state_in[1][at, :] * factor
            f2 = jnp.concatenate([factor, factor], axis=1)
            pair_sum = pair_sum + state_in[2][at, :] * f2
            accv[at, :] = state_in[3][at, :] * jnp.concatenate([f2, f2], axis=1)
        l_out[at, :] = part
        accp[at, :] = pair_sum

    w, full, tail = {}, {}, {}
    for step in range(8 + 3):
        if step < 8:
            w[step] = stage1(step)
        if 0 <= step - 1 < 8:
            full[step - 1] = stage2(w.pop(step - 1))
        if 0 <= step - 2 < 8:
            tail[step - 2] = stage3(step - 2, full.pop(step - 2))
        if 0 <= step - 3 < 8:
            stage4(step - 3, *tail.pop(step - 3))
    sums = dot_nt(wbuf[...], vt[...])
    accv[...] = sums if state_in is None else accv[...] + sums


def make_first(count):
    def first_kernel(*refs):
        attend(refs[:count], refs[count : count + 6], None, refs[count + 6 : count + 10], refs[count + 10 :])

    return first_kernel


def make_next(count):
    def next_kernel(*refs):
        attend(refs[:count], refs[count : count + 6], refs[count + 6 : count + 10], refs[count + 10 : count + 14], refs[count + 14 :])

    return next_kernel


def attend_cost(count):
    return pl.CostEstimate(flops=3_000_000_000 * count, bytes_accessed=4_000_000, transcendentals=600_000 * count)


def make_last(count):
    def last_kernel(*refs):
        ops = refs[count : count + 6]
        state_in = refs[count + 6 : count + 10]
        single_ref, fr_ref, frt_ref, wout_ref, gain_ref, wframe_ref, out_ref, frames_ref = refs[
            count + 10 : count + 18
        ]
        m_scr, l_scr, accp, accv, apair = refs[count + 18 : count + 23]
        scr = refs[count + 23 :]
        l0 = scr[1]
        attend(refs[:count], ops, state_in, (m_scr, l_scr, accp, accv), scr)
        inv = 1.0 / jnp.sum(l_scr[...], axis=1, keepdims=True)
        row = lax.broadcasted_iota(jnp.int32, (256, 128), 0)
        first = jnp.bitwise_and(row, 16) == 0
        col, head = iota((HPAD, 512), 1), iota((HPAD, 512), 0)
        own = jnp.where(col < 192, col >> 4, modulo(col, 96) >> 3)
        vmask = one_where((own == head) & (col < 480))
        for k in range(4):
            apair[...] = accv[:, 128 * k : 128 * (k + 1)] * inv
            total = None
            for h in range(HEADS):
                piece = apair[pl.ds(h, ROWS, stride=HPAD), :] * vmask[h : h + 1, 128 * k : 128 * (k + 1)]
                total = piece if total is None else total + piece
            l0[0:ROWS, 128 * k : 128 * (k + 1)] = total
        apair[...] = jnp.where(first, accp[:, 0:128], accp[:, 128:256]) * inv
        attv = l0[0:ROWS, 0:512]
        mixed = single_ref[...].astype(F32)
        mixed = mixed + dot(attv[:, 0:192].astype(BF16), wout_ref[0:192, :])
        fr = fr_ref[...]
        rel = [attv[:, 192 + 96 * y : 192 + 96 * (y + 1)] - fr[:, 9 + y : 10 + y] for y in range(3)]
        norm = None
        for x in range(3):
            local = fr[:, x : x + 1] * rel[0] + fr[:, 3 + x : 4 + x] * rel[1] + fr[:, 6 + x : 7 + x] * rel[2]
            norm = local * local if norm is None else norm + local * local
            mixed = mixed + dot(local.astype(BF16), wout_ref[192 + 96 * x : 192 + 96 * (x + 1), :])
        norm = jnp.sqrt(norm + 1e-08)
        mixed = mixed + dot(norm.astype(BF16), wout_ref[480:576, :])
        for h in range(HEADS):
            mixed = mixed + dot(
                apair[pl.ds(h, ROWS, stride=HPAD), :].astype(BF16), wout_ref[576 + 128 * h : 576 + 128 * (h + 1), :]
            )
        mean = jnp.mean(mixed, axis=1, keepdims=True)
        center = mixed - mean
        snew = center * lax.rsqrt(jnp.mean(center * center, axis=1, keepdims=True) + 1e-05) * gain_ref[...].reshape(1, CS)
        out_ref[...] = snew.astype(BF16)
        upd = lax.dot_general(
            wframe_ref[...], snew, (((1,), (1,)), ((), ())), preferred_element_type=F32, precision=HI
        )
        ub, uc, ud = upd[0:1, 0:ROWS], upd[1:2, 0:ROWS], upd[2:3, 0:ROWS]
        n = jnp.sqrt(1.0 + ub * ub + uc * uc + ud * ud)
        ua = 1.0 / n
        ub, uc, ud = ub / n, uc / n, ud / n
        ru = [
            [ua * ua + ub * ub - uc * uc - ud * ud, 2.0 * (ub * uc - ua * ud), 2.0 * (ub * ud + ua * uc)],
            [2.0 * (ub * uc + ua * ud), ua * ua - ub * ub + uc * uc - ud * ud, 2.0 * (uc * ud - ua * ub)],
            [2.0 * (ub * ud - ua * uc), 2.0 * (uc * ud + ua * ub), ua * ua - ub * ub - uc * uc + ud * ud],
        ]
        frt = frt_ref[...]
        rot = [[frt[3 * x + y : 3 * x + y + 1] for y in range(3)] for x in range(3)]
        res = []
        for x in range(3):
            for z in range(3):
                res.append(rot[x][0] * ru[0][z] + rot[x][1] * ru[1][z] + rot[x][2] * ru[2][z])
        for x in range(3):
            s = frt[9 + x : 10 + x]
            for y in range(3):
                s = s + rot[x][y] * upd[3 + y : 4 + y, 0:ROWS]
            res.append(s)
        frames_ref[...] = jnp.concatenate(res, axis=0)

    return last_kernel


STRIDE = {"z": 32, "x": 8, "y": 2}
FIRST = (("x", "y"), ("x", "z"))
SECOND = ("z", "y")


def plane_groups():
    groups = {}
    for d in range(128):
        key = d
        for axis in FIRST[d % 2]:
            key -= ((d // STRIDE[axis]) % 4) * STRIDE[axis]
        groups.setdefault(key, []).append(d)
    return list(groups.values())


def axis_perm(shift):
    perm = []
    for d in range(128):
        stride = STRIDE[SECOND[d % 2]]
        at = (d // stride) % 4
        perm.append((d, d + (((at + shift) % 4) - at) * stride))
    return perm


STATE = ((256, 128), (256, 128), (256, 256), (256, 512))
CORE = [(d, d ^ 1) for d in range(128)]


def attend_scratch(n):
    return [
        pltpu.VMEM((256, n), BF16),
        pltpu.VMEM((256, n), F32),
        pltpu.VMEM((512, n), BF16),
        pltpu.VMEM((K_ALL, n), BF16),
        pltpu.VMEM((256, n), BF16),
        pltpu.VMEM((8, 256, n), BF16),
        pltpu.VMEM((256, n), F32),
    ]


def per_device(
    single, angles, trans, left_factor, right_factor, chain, live,
    w_query, w_keyval, w_qpoints, w_kvpoints, w_pair_in, chain_bias, w_pair_out, w_bias,
    point_weight, w_out, out_gain, w_frame,
):
    vm = pl.BlockSpec(memory_space=pltpu.VMEM)
    packed, fr, frt = pl.pallas_call(
        pack_kernel,
        out_shape=(
            jax.ShapeDtypeStruct((PIECE, PACK), BF16),
            jax.ShapeDtypeStruct((ROWS, 128), F32),
            jax.ShapeDtypeStruct((16, ROWS), F32),
        ),
        in_specs=[vm] * 6,
        out_specs=(vm, vm, vm),
        cost_estimate=pl.CostEstimate(flops=4_000_000_000, bytes_accessed=8_000_000, transcendentals=1000),
    )(single, angles, trans, right_factor, chain[None], live[None])

    own = lax.all_to_all(packed, "blk", 0, 0, tiled=True, axis_index_groups=plane_groups())
    near = [own, lax.ppermute(own, "blk", CORE)]
    far = [lax.ppermute(own, "blk", axis_perm(s)) for s in (1, 3, 2)]

    near[1], single_q = lax.optimization_barrier((near[1], single))
    ops = pl.pallas_call(
        query_kernel,
        out_shape=(
            jax.ShapeDtypeStruct((256, K_ALL), BF16),
            jax.ShapeDtypeStruct((2048, 256), BF16),
            jax.ShapeDtypeStruct((320, 256), BF16),
            jax.ShapeDtypeStruct((R_ALL, PACK), BF16),
            jax.ShapeDtypeStruct((16, 128), F32),
            jax.ShapeDtypeStruct((HPAD, 144), BF16),
        ),
        in_specs=[vm] * 12,
        out_specs=(vm,) * 6,
        scratch_shapes=[pltpu.VMEM((ROWS, K_ALL), F32)],
        compiler_params=pltpu.CompilerParams(vmem_limit_bytes=16 << 20),
        cost_estimate=pl.CostEstimate(flops=600_000_000, bytes_accessed=5_000_000, transcendentals=0),
    )(
        single_q, fr, left_factor, w_query.T, w_qpoints.T, w_pair_in, chain_bias[None], w_pair_out, w_bias.T,
        point_weight[None], w_keyval, w_kvpoints.T,
    )
    scratch = [pltpu.VMEM(shape, F32) for shape in STATE]
    state = pl.pallas_call(
        make_first(len(near)),
        out_shape=tuple(jax.ShapeDtypeStruct(shape, F32) for shape in STATE),
        in_specs=[vm] * (len(near) + len(ops)),
        out_specs=(vm,) * 4,
        scratch_shapes=attend_scratch(PIECE * len(near)),
        compiler_params=pltpu.CompilerParams(vmem_limit_bytes=12 << 20),
        cost_estimate=attend_cost(len(near)),
    )(*near, *ops)
    far, state = lax.optimization_barrier((far, state))
    other = [lax.ppermute(piece, "blk", CORE) for piece in far]
    state = pl.pallas_call(
        make_next(len(far)),
        out_shape=tuple(jax.ShapeDtypeStruct(shape, F32) for shape in STATE),
        in_specs=[vm] * (len(far) + len(ops) + 4),
        out_specs=(vm,) * 4,
        scratch_shapes=attend_scratch(PIECE * len(far)),
        compiler_params=pltpu.CompilerParams(vmem_limit_bytes=20 << 20),
        cost_estimate=attend_cost(len(far)),
    )(*far, *ops, *state)
    out, frames = pl.pallas_call(
        make_last(len(other)),
        out_shape=(
            jax.ShapeDtypeStruct((ROWS, CS), BF16),
            jax.ShapeDtypeStruct((12, ROWS), F32),
        ),
        in_specs=[vm] * (len(other) + len(ops) + 4 + 6),
        out_specs=(vm, vm),
        scratch_shapes=scratch + [pltpu.VMEM((256, 128), F32)] + attend_scratch(PIECE * len(other)),
        compiler_params=pltpu.CompilerParams(vmem_limit_bytes=20 << 20),
        cost_estimate=attend_cost(len(other)),
    )(*other, *ops, *state, single, fr, frt, w_out, out_gain, w_frame.T)
    return out, frames


def solution(mesh):
    in_specs = (
        P("blk", None), P(None, "blk"), P(None, "blk"), P("blk", None), P("blk", None), P("blk"), P("blk"),
    ) + (P(),) * 12
    out_specs = (P("blk", None), P(None, "blk"))
    return jax.shard_map(per_device, mesh=mesh, in_specs=in_specs, out_specs=out_specs, check_vma=False)
```

```python
import math

import jax
import jax.numpy as jnp
from jax import lax
from jax.experimental import pallas as pl
from jax.experimental.pallas import tpu as pltpu
from jax.sharding import PartitionSpec as P

F32 = jnp.float32
BF16 = jnp.bfloat16
HI = lax.Precision.HIGHEST

HEADS, HD, QP, VP, CZ, RANK, CS = 12, 16, 4, 8, 128, 64, 384
ROWS = 16
HPAD = 16
PACK = 512
C_HI, C_MID, C_LO, C_CHAIN, C_LIVE = 64, 76, 88, 100, 108
R_VAL, R_KP, R_VP, R_SEL, R_TILE, R_ALL = 192, 384, 528, 816, 832, 960
K_P = (192, 336, 480)
K_ONE = 624
K_QSQ = 672
K_ALL = 768
C0 = math.sqrt(2.0 / math.pi)
GAMMA = (C0 * 0.044715) ** (1.0 / 3.0)
GB = C0 / GAMMA
S3 = math.sqrt(1.0 / 3.0)
PLANE = 16
PIECE = ROWS * PLANE
COEF = math.sqrt(2.0 / (9.0 * QP)) / 2.0


def dot(a, b):
    return jnp.dot(a, b, preferred_element_type=F32)


def dot_nt(a, b):
    return lax.dot_general(a, b, (((1,), (1,)), ((), ())), preferred_element_type=F32)


def dot_hi(a, b):
    return jnp.dot(a, b, preferred_element_type=F32, precision=HI)


def split3(x):
    hi = x.astype(BF16).astype(F32)
    mid = (x - hi).astype(BF16).astype(F32)
    low = (x - hi - mid).astype(BF16).astype(F32)
    return hi, mid, low


def square_pad(x):
    r, c = x.shape
    if c < 128:
        x = jnp.concatenate([x, jnp.zeros((r, 128 - c), x.dtype)], axis=1)
    if r < 128:
        x = jnp.concatenate([x, jnp.zeros((128 - r, 128), x.dtype)], axis=0)
    return x


def frame_rows(angles_ref, trans_ref, chain_ref, live_ref):
    ang = angles_ref[...]
    cosines, sines = jnp.cos(ang), jnp.sin(ang)
    ca, cb, cc = cosines[0:1], cosines[1:2], cosines[2:3]
    sa, sb, sc = sines[0:1], sines[1:2], sines[2:3]
    rows = [
        ca * cb, -sa * cc + ca * sb * sc, sa * sc + ca * sb * cc,
        sa * cb, ca * cc + sa * sb * sc, -ca * sc + sa * sb * cc,
        -sb, cb * sc, cb * cc,
    ]
    return jnp.concatenate(
        rows
        + [trans_ref[...], chain_ref[...].astype(F32), live_ref[...].astype(F32), jnp.zeros((2, ROWS), F32)],
        axis=0,
    )


def pack_kernel(single_ref, angles_ref, trans_ref, right_ref, chain_ref, live_ref, out_ref):
    wide = square_pad(frame_rows(angles_ref, trans_ref, chain_ref, live_ref)).T[0:ROWS]
    lane = lax.broadcasted_iota(jnp.int32, (ROWS, 128), 1)
    frame = jnp.where(lane < 12, wide, 0.0)
    hi, mid, low = split3(frame)
    tile = pltpu.roll(hi, C_HI, 1) + pltpu.roll(mid, C_MID, 1) + pltpu.roll(low, C_LO, 1)
    chain = wide[:, 12:13]
    live = wide[:, 13:14]
    tile = tile + jnp.where((lane - C_CHAIN).astype(F32) == chain, jnp.where(lane >= C_CHAIN, 1.0, 0.0), 0.0)
    tile = tile + jnp.where(lane == C_LIVE, live, 0.0)
    right = jnp.concatenate([right_ref[...].astype(F32), jnp.zeros((ROWS, 64), F32)], axis=1)
    row = single_ref[...]
    tile = (tile + right).astype(BF16)
    for k in range(PLANE):
        out_ref[ROWS * k : ROWS * (k + 1), 0:CS] = row
        out_ref[ROWS * k : ROWS * (k + 1), CS:PACK] = tile


def iota(shape, axis):
    return lax.broadcasted_iota(jnp.int32, shape, axis)


def modulo(x, m):
    return x - m * jnp.floor((x.astype(F32) + 0.5) * (1.0 / m)).astype(jnp.int32)


def one_where(condition):
    return jnp.where(condition, 1.0, 0.0)


def query_kernel(
    single_ref, angles_ref, trans_ref, chain_ref, live_ref, left_ref, wq_ref, wqp_ref, win_ref, cb_ref, wpo_ref, wb_ref,
    pw_ref, wkv_ref, wkvp_ref, a_ref, wall_ref, cmat_ref, wt_ref, coef_ref, ksum_ref, fr_ref, frt_ref, q_scr,
):
    rows = single_ref[...]
    query = dot_nt(rows, wq_ref[...]).astype(BF16).astype(F32)
    points = dot_nt(rows, wqp_ref[...])
    tall = frame_rows(angles_ref, trans_ref, chain_ref, live_ref)
    frt_ref[...] = tall
    fr = square_pad(tall).T[0:ROWS]
    fr_ref[...] = fr
    pts = [points[:, 48 * y : 48 * (y + 1)] for y in range(3)]
    coef = pw_ref[...] * COEF
    spread = dot_hi(coef, one_where(iota((HEADS, 48), 1) >> 2 == iota((HEADS, 48), 0)))
    q_scr[:, 0:192] = query
    sq = jnp.zeros((ROWS, 48), F32)
    for x in range(3):
        g = fr[:, 9 + x : 10 + x]
        g = g + (fr[:, 3 * x : 3 * x + 1] * pts[0] + fr[:, 3 * x + 1 : 3 * x + 2] * pts[1] + fr[:, 3 * x + 2 : 3 * x + 3] * pts[2])
        sq = sq + g * g
        parts = split3(g * (8.0 * spread))
        for k in range(3):
            q_scr[:, K_P[k] + 48 * x : K_P[k] + 48 * (x + 1)] = parts[k]
    qsq = dot_hi(sq * (-4.0 * spread), one_where(iota((48, HPAD), 0) >> 2 == iota((48, HPAD), 1)))
    q_scr[:, K_ONE:K_QSQ] = jnp.ones((ROWS, 48), F32)
    parts = split3(qsq)
    for k in range(3):
        q_scr[:, K_QSQ + 16 * k : K_QSQ + 16 * (k + 1)] = parts[k]
    q_scr[:, K_QSQ + 48 : K_ALL] = jnp.zeros((ROWS, K_ALL - K_QSQ - 48), F32)
    col, head = iota((HPAD, K_ALL), 1), iota((HPAD, K_ALL), 0)
    of_point = modulo(col, 48) >> 2
    own = jnp.where(col < 192, col >> 4, jnp.where(col < K_ONE, of_point, jnp.bitwise_and(col, 15)))
    mask = one_where((own == head) & (head < HEADS) & (col < K_QSQ + 48))
    for i in range(ROWS):
        a_ref[i * HPAD : (i + 1) * HPAD, :] = (q_scr[i : i + 1, :] * mask).astype(BF16)
    win_t = square_pad(win_ref[...].astype(F32)).T * GAMMA
    cb = cb_ref[...] * GAMMA
    cb_t = square_pad(cb).T[:, 0:1]
    lane = lax.broadcasted_iota(jnp.int32, (128, 128), 1).astype(F32)
    left = left_ref[...].astype(F32)
    left = jnp.concatenate([left, jnp.zeros((ROWS, 64), F32)], axis=1)
    for i in range(ROWS):
        w = win_t * left[i : i + 1, :]
        w = w + jnp.where(lane == fr[i : i + 1, 12:13] + C_CHAIN, cb_t, 0.0)
        hi = w.astype(BF16)
        wall_ref[i * 128 : (i + 1) * 128, 0:128] = hi
        wall_ref[i * 128 : (i + 1) * 128, 128:256] = (w - hi.astype(F32)).astype(BF16)
    w = wpo_ref[...].astype(F32)
    w = (w - jnp.mean(w, axis=1, keepdims=True)) * (0.5 / GAMMA)
    wb_t = jnp.concatenate([wb_ref[...].astype(F32), jnp.zeros((HPAD - HEADS, CZ), F32)], axis=0)
    w_t = w.T
    both = dot_hi(wb_t, w_t)
    hi = both.astype(BF16)
    low = (both - hi.astype(F32)).astype(BF16)
    cmat_ref[...] = jnp.zeros((320, 256), BF16)
    for k in range(2):
        lanes = slice(128 * k, 128 * (k + 1))
        cmat_ref[lanes, lanes] = w_t.astype(BF16)
        cmat_ref[256 + 16 * k : 272 + 16 * k, lanes] = hi
        cmat_ref[288 + 16 * k : 304 + 16 * k, lanes] = low
    wt_ref[0:384, 0:CS] = wkv_ref[...].astype(F32).T.astype(BF16)
    row = iota((432, 432), 0)
    is_key = row < 144
    val = row - 144
    axis = jnp.where(is_key, one_where(row >= 48) + one_where(row >= 96), one_where(val >= 96) + one_where(val >= 192))
    axis = axis.astype(jnp.int32)
    key_at, val_at = row - 48 * axis, val - 96 * axis
    source = jnp.where(
        is_key,
        (key_at >> 2) * (QP + VP) + jnp.bitwise_and(key_at, 3),
        (val_at >> 3) * (QP + VP) + QP + jnp.bitwise_and(val_at, 7),
    )
    perm = one_where(source + 144 * axis == iota((432, 432), 1)).astype(BF16)
    wt_ref[384:816, 0:CS] = dot(perm, wkvp_ref[...]).astype(BF16)
    wt_ref[0:R_ALL, CS:PACK] = jnp.zeros((R_ALL, PACK - CS), BF16)
    wt_ref[R_SEL:R_ALL, 0:CS] = jnp.zeros((R_ALL - R_SEL, CS), BF16)
    row, col = iota((16, 128), 0), iota((16, 128), 1)
    sel = (row < 12) & ((col - row == C_HI) | (col - row == C_MID) | (col - row == C_LO))
    sel = sel | ((row == 12) & (col == C_LIVE))
    wt_ref[R_SEL:R_TILE, CS:PACK] = one_where(sel).astype(BF16)
    wt_ref[R_TILE:R_ALL, CS:PACK] = one_where(iota((128, 128), 0) == iota((128, 128), 1)).astype(BF16)
    ksum_ref[...] = one_where(modulo(iota((HPAD, 144), 1), 48) >> 2 == iota((HPAD, 144), 0)).astype(BF16)
    sub = lax.broadcasted_iota(jnp.int32, (16, HEADS), 0)
    col = lax.broadcasted_iota(jnp.int32, (16, HEADS), 1)
    coef_ref[...] = jnp.broadcast_to(
        jnp.sum(jnp.where(sub == col, -4.0 * coef, 0.0), axis=1, keepdims=True), (16, 128)
    )


def attend(pieces, ops, state_in, state_out, scr):
    a_ref, wall_ref, cmat_ref, wt_ref, coef_ref, ksum_ref = ops
    m_out, l_out, accp, accv = state_out
    wbuf, l0, vt, bmat, wide, cbuf, rsbuf = scr
    n = PIECE * len(pieces)
    vt[480:512, :] = jnp.zeros((32, n), BF16)
    bmat[K_QSQ:K_ALL, :] = jnp.ones((K_ALL - K_QSQ, n), BF16)
    coef = coef_ref[:, 0:1]
    rows = jnp.concatenate([piece[...] for piece in pieces], axis=0)
    for at in (slice(0, n),):
        kvt = dot_nt(wt_ref[0:R_SEL, 0:CS], rows[:, 0:CS])
        low = dot_nt(wt_ref[R_SEL:R_ALL, CS:PACK], rows[:, CS:PACK])
        tile = low[R_TILE - R_SEL :].astype(BF16)
        wide[0:128, at] = tile
        wide[128:256, at] = tile
        bmat[0:192, at] = kvt[0:192].astype(BF16)
        vt[0:192, at] = kvt[R_VAL : R_VAL + 192].astype(BF16)
        sel = low[0:16]
        ksq = None
        for x in range(3):
            r = [sel[3 * x + y : 3 * x + y + 1] for y in range(3)]
            t = sel[9 + x : 10 + x]
            kp = t
            vp = t
            for y in range(3):
                kp = kp + r[y] * kvt[R_KP + 48 * y : R_KP + 48 * (y + 1)]
                vp = vp + r[y] * kvt[R_VP + 96 * y : R_VP + 96 * (y + 1)]
            kb = kp.astype(BF16)
            for k in range(3):
                bmat[K_P[k] + 48 * x : K_P[k] + 48 * (x + 1), at] = kb
            vt[192 + 96 * x : 192 + 96 * (x + 1), at] = vp.astype(BF16)
            kf = kb.astype(F32)
            ksq = kf * kf if ksq is None else ksq + kf * kf
        hi, mid, lo = split3(ksq)
        ks = dot(ksum_ref[...], jnp.concatenate([hi, mid, lo], axis=0).astype(BF16))
        dead = 100000.0 * (1.0 - sel[12:13])
        ks = ks * coef - (4.0 / S3) * dead
        hi, mid, lo = split3(ks)
        bmat[K_ONE : K_ONE + 48, at] = jnp.concatenate([hi, mid, lo], axis=0).astype(BF16)
    l0[...] = dot(a_ref[...], bmat[...]) * (S3 / 4.0)

    def stage1(p):
        return dot(wall_ref[p * 256 : (p + 1) * 256, :], wide[...])

    def stage2(w):
        t = jnp.tanh(w * (w * w + GB))
        hid = (w + w * t).astype(BF16)
        return dot(cmat_ref[...], hid)

    def stage3(p, full):
        at = slice(p * 32, (p + 1) * 32)
        center = full[0:256]
        cb = center.astype(BF16)
        sq = center * center
        rs = []
        for k in range(2):
            var = jnp.sum(sq[128 * k : 128 * (k + 1)], axis=0, keepdims=True) * (1.0 / CZ)
            rs.append(jnp.broadcast_to(lax.rsqrt(var + 1e-05), (16, n)))
        rs = jnp.concatenate(rs, axis=0)
        logits = l0[at, :] + (full[256:288] + full[288:320]) * (rs * S3)
        new = jnp.max(logits, axis=1, keepdims=True)
        factor = None
        if state_in is not None:
            top = state_in[0][at, :]
            new = jnp.maximum(top, new)
            factor = jnp.exp(top - new)
        terms = jnp.exp(logits - new[:, 0:1])
        m_out[at, :] = jnp.broadcast_to(new, (32, 128))
        part = terms[:, 0:128]
        for k in range(1, n // 128):
            part = part + terms[:, 128 * k : 128 * (k + 1)]
        wbuf[at, :] = terms.astype(BF16)
        return cb, (terms * rs).astype(BF16), part, factor

    def stage4(p, cb, wr, part, factor):
        at = slice(p * 32, (p + 1) * 32)
        pair_sum = dot_nt(wr, cb)
        if state_in is not None:
            part = part + state_in[1][at, :] * factor
            f2 = jnp.concatenate([factor, factor], axis=1)
            pair_sum = pair_sum + state_in[2][at, :] * f2
            accv[at, :] = state_in[3][at, :] * jnp.concatenate([f2, f2], axis=1)
        l_out[at, :] = part
        accp[at, :] = pair_sum

    w, full, tail = {}, {}, {}
    for step in range(8 + 3):
        if step < 8:
            w[step] = stage1(step)
        if 0 <= step - 1 < 8:
            full[step - 1] = stage2(w.pop(step - 1))
        if 0 <= step - 2 < 8:
            tail[step - 2] = stage3(step - 2, full.pop(step - 2))
        if 0 <= step - 3 < 8:
            stage4(step - 3, *tail.pop(step - 3))
    sums = dot_nt(wbuf[...], vt[...])
    accv[...] = sums if state_in is None else accv[...] + sums


def make_first(count):
    def first_kernel(*refs):
        attend(refs[:count], refs[count : count + 6], None, refs[count + 6 : count + 10], refs[count + 10 :])

    return first_kernel


def make_next(count):
    def next_kernel(*refs):
        attend(refs[:count], refs[count : count + 6], refs[count + 6 : count + 10], refs[count + 10 : count + 14], refs[count + 14 :])

    return next_kernel


def attend_cost(count):
    return pl.CostEstimate(flops=3_000_000_000 * count, bytes_accessed=4_000_000, transcendentals=600_000 * count)


def make_last(count):
    def last_kernel(*refs):
        ops = refs[count : count + 6]
        state_in = refs[count + 6 : count + 10]
        single_ref, fr_ref, frt_ref, wout_ref, gain_ref, wframe_ref, out_ref, frames_ref = refs[
            count + 10 : count + 18
        ]
        m_scr, l_scr, accp, accv, apair, feats = refs[count + 18 : count + 24]
        scr = refs[count + 24 :]
        attend(refs[:count], ops, state_in, (m_scr, l_scr, accp, accv), scr)
        inv = 1.0 / jnp.sum(l_scr[...], axis=1, keepdims=True)
        row = lax.broadcasted_iota(jnp.int32, (256, 128), 0)
        first = jnp.bitwise_and(row, 16) == 0
        col, head = iota((HPAD, 512), 1), iota((HPAD, 512), 0)
        own = jnp.where(col < 192, col >> 4, modulo(col, 96) >> 3)
        vmask = one_where((own == head) & (col < 480))
        attv = jnp.sum((accv[...] * inv).reshape(ROWS, HPAD, 512) * vmask[None], axis=1)
        apair[...] = jnp.where(first, accp[:, 0:128], accp[:, 128:256]) * inv
        feats[:, 0:192] = attv[:, 0:192]
        fr = fr_ref[...]
        rel = [attv[:, 192 + 96 * y : 192 + 96 * (y + 1)] - fr[:, 9 + y : 10 + y] for y in range(3)]
        norm = None
        for x in range(3):
            local = fr[:, x : x + 1] * rel[0] + fr[:, 3 + x : 4 + x] * rel[1] + fr[:, 6 + x : 7 + x] * rel[2]
            norm = local * local if norm is None else norm + local * local
            feats[:, 192 + 96 * x : 192 + 96 * (x + 1)] = local
        feats[:, 480:576] = jnp.sqrt(norm + 1e-08)
        wide = jnp.concatenate([apair[pl.ds(h, ROWS, stride=HPAD), :] for h in range(HEADS)], axis=1).astype(BF16)
        mixed = single_ref[...].astype(F32) + dot(wide, wout_ref[576:2112, :])
        mixed = mixed + dot(feats[...].astype(BF16), wout_ref[0:576, :])
        mean = jnp.mean(mixed, axis=1, keepdims=True)
        center = mixed - mean
        snew = center * lax.rsqrt(jnp.mean(center * center, axis=1, keepdims=True) + 1e-05) * gain_ref[...].reshape(1, CS)
        out_ref[...] = snew.astype(BF16)
        upd = lax.dot_general(
            wframe_ref[...], snew, (((1,), (1,)), ((), ())), preferred_element_type=F32, precision=HI
        )
        ub, uc, ud = upd[0:1, 0:ROWS], upd[1:2, 0:ROWS], upd[2:3, 0:ROWS]
        n = jnp.sqrt(1.0 + ub * ub + uc * uc + ud * ud)
        ua = 1.0 / n
        ub, uc, ud = ub / n, uc / n, ud / n
        ru = [
            [ua * ua + ub * ub - uc * uc - ud * ud, 2.0 * (ub * uc - ua * ud), 2.0 * (ub * ud + ua * uc)],
            [2.0 * (ub * uc + ua * ud), ua * ua - ub * ub + uc * uc - ud * ud, 2.0 * (uc * ud - ua * ub)],
            [2.0 * (ub * ud - ua * uc), 2.0 * (uc * ud + ua * ub), ua * ua - ub * ub - uc * uc + ud * ud],
        ]
        frt = frt_ref[...]
        rot = [[frt[3 * x + y : 3 * x + y + 1] for y in range(3)] for x in range(3)]
        res = []
        for x in range(3):
            for z in range(3):
                res.append(rot[x][0] * ru[0][z] + rot[x][1] * ru[1][z] + rot[x][2] * ru[2][z])
        for x in range(3):
            s = frt[9 + x : 10 + x]
            for y in range(3):
                s = s + rot[x][y] * upd[3 + y : 4 + y, 0:ROWS]
            res.append(s)
        frames_ref[...] = jnp.concatenate(res, axis=0)

    return last_kernel


STRIDE = {"z": 32, "x": 8, "y": 2}
FIRST = (("x", "y"), ("x", "z"))
SECOND = ("z", "y")


def plane_groups():
    groups = {}
    for d in range(128):
        key = d
        for axis in FIRST[d % 2]:
            key -= ((d // STRIDE[axis]) % 4) * STRIDE[axis]
        groups.setdefault(key, []).append(d)
    return list(groups.values())


def axis_perm(shift):
    perm = []
    for d in range(128):
        stride = STRIDE[SECOND[d % 2]]
        at = (d // stride) % 4
        perm.append((d, d + (((at + shift) % 4) - at) * stride))
    return perm


STATE = ((256, 128), (256, 128), (256, 256), (256, 512))
CORE = [(d, d ^ 1) for d in range(128)]


def attend_scratch(n):
    return [
        pltpu.VMEM((256, n), BF16),
        pltpu.VMEM((256, n), F32),
        pltpu.VMEM((512, n), BF16),
        pltpu.VMEM((K_ALL, n), BF16),
        pltpu.VMEM((256, n), BF16),
        pltpu.VMEM((8, 256, n), BF16),
        pltpu.VMEM((256, n), F32),
    ]


def per_device(
    single, angles, trans, left_factor, right_factor, chain, live,
    w_query, w_keyval, w_qpoints, w_kvpoints, w_pair_in, chain_bias, w_pair_out, w_bias,
    point_weight, w_out, out_gain, w_frame,
):
    vm = pl.BlockSpec(memory_space=pltpu.VMEM)
    packed = pl.pallas_call(
        pack_kernel,
        out_shape=jax.ShapeDtypeStruct((PIECE, PACK), BF16),
        in_specs=[vm] * 6,
        out_specs=vm,
        cost_estimate=pl.CostEstimate(flops=4_000_000_000, bytes_accessed=8_000_000, transcendentals=1000),
    )(single, angles, trans, right_factor, chain[None], live[None])

    own = lax.all_to_all(packed, "blk", 0, 0, tiled=True, axis_index_groups=plane_groups())
    near = [own, lax.ppermute(own, "blk", CORE)]
    far = [lax.ppermute(own, "blk", axis_perm(s)) for s in (2, 3, 1)]

    near[1], single_q = lax.optimization_barrier((near[1], single))
    *ops, fr, frt = pl.pallas_call(
        query_kernel,
        out_shape=(
            jax.ShapeDtypeStruct((256, K_ALL), BF16),
            jax.ShapeDtypeStruct((2048, 256), BF16),
            jax.ShapeDtypeStruct((320, 256), BF16),
            jax.ShapeDtypeStruct((R_ALL, PACK), BF16),
            jax.ShapeDtypeStruct((16, 128), F32),
            jax.ShapeDtypeStruct((HPAD, 144), BF16),
            jax.ShapeDtypeStruct((ROWS, 128), F32),
            jax.ShapeDtypeStruct((16, ROWS), F32),
        ),
        in_specs=[vm] * 15,
        out_specs=(vm,) * 8,
        scratch_shapes=[pltpu.VMEM((ROWS, K_ALL), F32)],
        compiler_params=pltpu.CompilerParams(vmem_limit_bytes=16 << 20),
        cost_estimate=pl.CostEstimate(flops=600_000_000, bytes_accessed=5_000_000, transcendentals=0),
    )(
        single_q, angles, trans, chain[None], live[None], left_factor, w_query.T, w_qpoints.T, w_pair_in, chain_bias[None], w_pair_out, w_bias.T,
        point_weight[None], w_keyval, w_kvpoints.T,
    )
    scratch = [pltpu.VMEM(shape, F32) for shape in STATE]
    state = pl.pallas_call(
        make_first(len(near)),
        out_shape=tuple(jax.ShapeDtypeStruct(shape, F32) for shape in STATE),
        in_specs=[vm] * (len(near) + len(ops)),
        out_specs=(vm,) * 4,
        scratch_shapes=attend_scratch(PIECE * len(near)),
        compiler_params=pltpu.CompilerParams(vmem_limit_bytes=12 << 20),
        cost_estimate=attend_cost(len(near)),
    )(*near, *ops)
    def further(taken, state):
        return pl.pallas_call(
            make_next(len(taken)),
            out_shape=tuple(jax.ShapeDtypeStruct(shape, F32) for shape in STATE),
            in_specs=[vm] * (len(taken) + len(ops) + 4),
            out_specs=(vm,) * 4,
            scratch_shapes=attend_scratch(PIECE * len(taken)),
            compiler_params=pltpu.CompilerParams(vmem_limit_bytes=20 << 20),
            cost_estimate=attend_cost(len(taken)),
        )(*taken, *ops, *state)

    early, state = lax.optimization_barrier((far[2], state))
    state = further([early], state)
    late, early, state = lax.optimization_barrier((far[:2], early, state))
    other = [lax.ppermute(piece, "blk", CORE) for piece in [early] + late]
    state = further(late, state)
    out, frames = pl.pallas_call(
        make_last(len(other)),
        out_shape=(
            jax.ShapeDtypeStruct((ROWS, CS), BF16),
            jax.ShapeDtypeStruct((12, ROWS), F32),
        ),
        in_specs=[vm] * (len(other) + len(ops) + 4 + 6),
        out_specs=(vm, vm),
        scratch_shapes=scratch + [pltpu.VMEM((256, 128), F32), pltpu.VMEM((ROWS, 576), F32)] + attend_scratch(PIECE * len(other)),
        compiler_params=pltpu.CompilerParams(vmem_limit_bytes=20 << 20),
        cost_estimate=attend_cost(len(other)),
    )(*other, *ops, *state, single, fr, frt, w_out, out_gain, w_frame.T)
    return out, frames


def solution(mesh):
    in_specs = (
        P("blk", None), P(None, "blk"), P(None, "blk"), P("blk", None), P("blk", None), P("blk"), P("blk"),
    ) + (P(),) * 12
    out_specs = (P("blk", None), P(None, "blk"))
    return jax.shard_map(per_device, mesh=mesh, in_specs=in_specs, out_specs=out_specs, check_vma=False)
```

```python
import math

import jax
import jax.numpy as jnp
from jax import lax
from jax.experimental import pallas as pl
from jax.experimental.pallas import tpu as pltpu
from jax.sharding import PartitionSpec as P

F32 = jnp.float32
BF16 = jnp.bfloat16
HI = lax.Precision.HIGHEST

HEADS, HD, QP, VP, CZ, RANK, CS = 12, 16, 4, 8, 128, 64, 384
ROWS = 16
HPAD = 16
PACK = 512
C_HI, C_MID, C_LO, C_CHAIN, C_LIVE = 64, 76, 88, 100, 108
R_VAL, R_KP, R_VP, R_SEL, R_TILE, R_ALL = 192, 384, 528, 816, 832, 960
K_P = (192, 336, 480)
K_ONE = 624
K_QSQ = 672
K_ALL = 768
C0 = math.sqrt(2.0 / math.pi)
GAMMA = (C0 * 0.044715) ** (1.0 / 3.0)
GB = C0 / GAMMA
S3 = math.sqrt(1.0 / 3.0)
PLANE = 32
PIECE = ROWS * PLANE
COEF = math.sqrt(2.0 / (9.0 * QP)) / 2.0


def dot(a, b):
    return jnp.dot(a, b, preferred_element_type=F32)


def dot_nt(a, b):
    return lax.dot_general(a, b, (((1,), (1,)), ((), ())), preferred_element_type=F32)


def dot_hi(a, b):
    return jnp.dot(a, b, preferred_element_type=F32, precision=HI)


def split3(x):
    hi = x.astype(BF16).astype(F32)
    mid = (x - hi).astype(BF16).astype(F32)
    low = (x - hi - mid).astype(BF16).astype(F32)
    return hi, mid, low


def square_pad(x):
    r, c = x.shape
    if c < 128:
        x = jnp.concatenate([x, jnp.zeros((r, 128 - c), x.dtype)], axis=1)
    if r < 128:
        x = jnp.concatenate([x, jnp.zeros((128 - r, 128), x.dtype)], axis=0)
    return x


def frame_rows(angles_ref, trans_ref, chain_ref, live_ref):
    ang = angles_ref[...]
    cosines, sines = jnp.cos(ang), jnp.sin(ang)
    ca, cb, cc = cosines[0:1], cosines[1:2], cosines[2:3]
    sa, sb, sc = sines[0:1], sines[1:2], sines[2:3]
    rows = [
        ca * cb, -sa * cc + ca * sb * sc, sa * sc + ca * sb * cc,
        sa * cb, ca * cc + sa * sb * sc, -ca * sc + sa * sb * cc,
        -sb, cb * sc, cb * cc,
    ]
    return jnp.concatenate(
        rows
        + [trans_ref[...], chain_ref[...].astype(F32), live_ref[...].astype(F32), jnp.zeros((2, ROWS), F32)],
        axis=0,
    )


def pack_kernel(single_ref, angles_ref, trans_ref, right_ref, chain_ref, live_ref, out_ref):
    wide = square_pad(frame_rows(angles_ref, trans_ref, chain_ref, live_ref)).T[0:ROWS]
    lane = lax.broadcasted_iota(jnp.int32, (ROWS, 128), 1)
    frame = jnp.where(lane < 12, wide, 0.0)
    hi, mid, low = split3(frame)
    tile = pltpu.roll(hi, C_HI, 1) + pltpu.roll(mid, C_MID, 1) + pltpu.roll(low, C_LO, 1)
    chain = wide[:, 12:13]
    live = wide[:, 13:14]
    tile = tile + jnp.where((lane - C_CHAIN).astype(F32) == chain, jnp.where(lane >= C_CHAIN, 1.0, 0.0), 0.0)
    tile = tile + jnp.where(lane == C_LIVE, live, 0.0)
    right = jnp.concatenate([right_ref[...].astype(F32), jnp.zeros((ROWS, 64), F32)], axis=1)
    row = single_ref[...]
    tile = (tile + right).astype(BF16)
    for k in range(PLANE):
        out_ref[ROWS * k : ROWS * (k + 1), 0:CS] = row
        out_ref[ROWS * k : ROWS * (k + 1), CS:PACK] = tile


def iota(shape, axis):
    return lax.broadcasted_iota(jnp.int32, shape, axis)


def modulo(x, m):
    return x - m * jnp.floor((x.astype(F32) + 0.5) * (1.0 / m)).astype(jnp.int32)


def one_where(condition):
    return jnp.where(condition, 1.0, 0.0)


def query_kernel(
    single_ref, angles_ref, trans_ref, chain_ref, live_ref, left_ref, wq_ref, wqp_ref, win_ref, cb_ref, wpo_ref, wb_ref,
    pw_ref, wkv_ref, wkvp_ref, a_ref, wall_ref, cmat_ref, wt_ref, coef_ref, ksum_ref, fr_ref, frt_ref, q_scr,
):
    rows = single_ref[...]
    query = dot_nt(rows, wq_ref[...]).astype(BF16).astype(F32)
    points = dot_nt(rows, wqp_ref[...])
    tall = frame_rows(angles_ref, trans_ref, chain_ref, live_ref)
    frt_ref[...] = tall
    fr = square_pad(tall).T[0:ROWS]
    fr_ref[...] = fr
    pts = [points[:, 48 * y : 48 * (y + 1)] for y in range(3)]
    coef = pw_ref[...] * COEF
    spread = dot_hi(coef, one_where(iota((HEADS, 48), 1) >> 2 == iota((HEADS, 48), 0)))
    q_scr[:, 0:192] = query
    sq = jnp.zeros((ROWS, 48), F32)
    for x in range(3):
        g = fr[:, 9 + x : 10 + x]
        g = g + (fr[:, 3 * x : 3 * x + 1] * pts[0] + fr[:, 3 * x + 1 : 3 * x + 2] * pts[1] + fr[:, 3 * x + 2 : 3 * x + 3] * pts[2])
        sq = sq + g * g
        parts = split3(g * (8.0 * spread))
        for k in range(3):
            q_scr[:, K_P[k] + 48 * x : K_P[k] + 48 * (x + 1)] = parts[k]
    qsq = dot_hi(sq * (-4.0 * spread), one_where(iota((48, HPAD), 0) >> 2 == iota((48, HPAD), 1)))
    q_scr[:, K_ONE:K_QSQ] = jnp.ones((ROWS, 48), F32)
    parts = split3(qsq)
    for k in range(3):
        q_scr[:, K_QSQ + 16 * k : K_QSQ + 16 * (k + 1)] = parts[k]
    q_scr[:, K_QSQ + 48 : K_ALL] = jnp.zeros((ROWS, K_ALL - K_QSQ - 48), F32)
    col, head = iota((HPAD, K_ALL), 1), iota((HPAD, K_ALL), 0)
    of_point = modulo(col, 48) >> 2
    own = jnp.where(col < 192, col >> 4, jnp.where(col < K_ONE, of_point, jnp.bitwise_and(col, 15)))
    mask = one_where((own == head) & (head < HEADS) & (col < K_QSQ + 48))
    for i in range(ROWS):
        a_ref[i * HPAD : (i + 1) * HPAD, :] = (q_scr[i : i + 1, :] * mask).astype(BF16)
    win_t = square_pad(win_ref[...].astype(F32)).T * GAMMA
    cb = cb_ref[...] * GAMMA
    cb_t = square_pad(cb).T[:, 0:1]
    lane = lax.broadcasted_iota(jnp.int32, (128, 128), 1).astype(F32)
    left = left_ref[...].astype(F32)
    left = jnp.concatenate([left, jnp.zeros((ROWS, 64), F32)], axis=1)
    for i in range(ROWS):
        w = win_t * left[i : i + 1, :]
        w = w + jnp.where(lane == fr[i : i + 1, 12:13] + C_CHAIN, cb_t, 0.0)
        hi = w.astype(BF16)
        wall_ref[i * 128 : (i + 1) * 128, 0:128] = hi
        wall_ref[i * 128 : (i + 1) * 128, 128:256] = (w - hi.astype(F32)).astype(BF16)
    w = wpo_ref[...].astype(F32)
    w = (w - jnp.mean(w, axis=1, keepdims=True)) * (0.5 / GAMMA)
    wb_t = jnp.concatenate([wb_ref[...].astype(F32), jnp.zeros((HPAD - HEADS, CZ), F32)], axis=0)
    w_t = w.T
    both = dot_hi(wb_t, w_t)
    hi = both.astype(BF16)
    low = (both - hi.astype(F32)).astype(BF16)
    cmat_ref[...] = jnp.zeros((320, 256), BF16)
    for k in range(2):
        lanes = slice(128 * k, 128 * (k + 1))
        cmat_ref[lanes, lanes] = w_t.astype(BF16)
        cmat_ref[256 + 16 * k : 272 + 16 * k, lanes] = hi
        cmat_ref[288 + 16 * k : 304 + 16 * k, lanes] = low
    wt_ref[0:384, 0:CS] = wkv_ref[...].astype(F32).T.astype(BF16)
    row = iota((432, 432), 0)
    is_key = row < 144
    val = row - 144
    axis = jnp.where(is_key, one_where(row >= 48) + one_where(row >= 96), one_where(val >= 96) + one_where(val >= 192))
    axis = axis.astype(jnp.int32)
    key_at, val_at = row - 48 * axis, val - 96 * axis
    source = jnp.where(
        is_key,
        (key_at >> 2) * (QP + VP) + jnp.bitwise_and(key_at, 3),
        (val_at >> 3) * (QP + VP) + QP + jnp.bitwise_and(val_at, 7),
    )
    perm = one_where(source + 144 * axis == iota((432, 432), 1)).astype(BF16)
    wt_ref[384:816, 0:CS] = dot(perm, wkvp_ref[...]).astype(BF16)
    wt_ref[0:R_ALL, CS:PACK] = jnp.zeros((R_ALL, PACK - CS), BF16)
    wt_ref[R_SEL:R_ALL, 0:CS] = jnp.zeros((R_ALL - R_SEL, CS), BF16)
    row, col = iota((16, 128), 0), iota((16, 128), 1)
    sel = (row < 12) & ((col - row == C_HI) | (col - row == C_MID) | (col - row == C_LO))
    sel = sel | ((row == 12) & (col == C_LIVE))
    wt_ref[R_SEL:R_TILE, CS:PACK] = one_where(sel).astype(BF16)
    wt_ref[R_TILE:R_ALL, CS:PACK] = one_where(iota((128, 128), 0) == iota((128, 128), 1)).astype(BF16)
    ksum_ref[...] = one_where(modulo(iota((HPAD, 144), 1), 48) >> 2 == iota((HPAD, 144), 0)).astype(BF16)
    sub = lax.broadcasted_iota(jnp.int32, (16, HEADS), 0)
    col = lax.broadcasted_iota(jnp.int32, (16, HEADS), 1)
    coef_ref[...] = jnp.broadcast_to(
        jnp.sum(jnp.where(sub == col, -4.0 * coef, 0.0), axis=1, keepdims=True), (16, 128)
    )


def attend(pieces, ops, state_in, state_out, scr):
    a_ref, wall_ref, cmat_ref, wt_ref, coef_ref, ksum_ref = ops
    m_out, l_out, accp, accv = state_out
    wbuf, l0, vt, bmat, wide = scr
    n = PIECE * len(pieces)
    vt[480:512, :] = jnp.zeros((32, n), BF16)
    bmat[K_QSQ:K_ALL, :] = jnp.ones((K_ALL - K_QSQ, n), BF16)
    coef = coef_ref[:, 0:1]
    rows = jnp.concatenate([piece[...] for piece in pieces], axis=0)
    for at in (slice(0, n),):
        kvt = dot_nt(wt_ref[0:R_SEL, 0:CS], rows[:, 0:CS])
        low = dot_nt(wt_ref[R_SEL:R_ALL, CS:PACK], rows[:, CS:PACK])
        tile = low[R_TILE - R_SEL :].astype(BF16)
        wide[0:128, at] = tile
        wide[128:256, at] = tile
        bmat[0:192, at] = kvt[0:192].astype(BF16)
        vt[0:192, at] = kvt[R_VAL : R_VAL + 192].astype(BF16)
        sel = low[0:16]
        ksq = None
        for x in range(3):
            r = [sel[3 * x + y : 3 * x + y + 1] for y in range(3)]
            t = sel[9 + x : 10 + x]
            kp = t
            vp = t
            for y in range(3):
                kp = kp + r[y] * kvt[R_KP + 48 * y : R_KP + 48 * (y + 1)]
                vp = vp + r[y] * kvt[R_VP + 96 * y : R_VP + 96 * (y + 1)]
            kb = kp.astype(BF16)
            for k in range(3):
                bmat[K_P[k] + 48 * x : K_P[k] + 48 * (x + 1), at] = kb
            vt[192 + 96 * x : 192 + 96 * (x + 1), at] = vp.astype(BF16)
            kf = kb.astype(F32)
            ksq = kf * kf if ksq is None else ksq + kf * kf
        hi, mid, lo = split3(ksq)
        ks = dot(ksum_ref[...], jnp.concatenate([hi, mid, lo], axis=0).astype(BF16))
        dead = 100000.0 * (1.0 - sel[12:13])
        ks = ks * coef - (4.0 / S3) * dead
        hi, mid, lo = split3(ks)
        bmat[K_ONE : K_ONE + 48, at] = jnp.concatenate([hi, mid, lo], axis=0).astype(BF16)
    l0[...] = dot(a_ref[...], bmat[...]) * (S3 / 4.0)

    def stage1(p):
        return dot(wall_ref[p * 256 : (p + 1) * 256, :], wide[...])

    def stage2(w):
        t = jnp.tanh(w * (w * w + GB))
        hid = (w + w * t).astype(BF16)
        return dot(cmat_ref[...], hid)

    def stage3(p, full):
        at = slice(p * 32, (p + 1) * 32)
        center = full[0:256]
        cb = center.astype(BF16)
        sq = center * center
        rs = []
        for k in range(2):
            var = jnp.sum(sq[128 * k : 128 * (k + 1)], axis=0, keepdims=True) * (1.0 / CZ)
            rs.append(jnp.broadcast_to(lax.rsqrt(var + 1e-05), (16, n)))
        rs = jnp.concatenate(rs, axis=0)
        logits = l0[at, :] + (full[256:288] + full[288:320]) * (rs * S3)
        new = jnp.max(logits, axis=1, keepdims=True)
        factor = None
        if state_in is not None:
            top = state_in[0][at, :]
            new = jnp.maximum(top, new)
            factor = jnp.exp(top - new)
        terms = jnp.exp(logits - new[:, 0:1])
        m_out[at, :] = jnp.broadcast_to(new, (32, 128))
        part = terms[:, 0:128]
        for k in range(1, n // 128):
            part = part + terms[:, 128 * k : 128 * (k + 1)]
        wbuf[at, :] = terms.astype(BF16)
        return cb, (terms * rs).astype(BF16), part, factor

    def stage4(p, cb, wr, part, factor):
        at = slice(p * 32, (p + 1) * 32)
        pair_sum = dot_nt(wr, cb)
        if state_in is not None:
            part = part + state_in[1][at, :] * factor
            f2 = jnp.concatenate([factor, factor], axis=1)
            pair_sum = pair_sum + state_in[2][at, :] * f2
            accv[at, :] = state_in[3][at, :] * jnp.concatenate([f2, f2], axis=1)
        l_out[at, :] = part
        accp[at, :] = pair_sum

    w, full, tail = {}, {}, {}
    for step in range(8 + 3):
        if step < 8:
            w[step] = stage1(step)
        if 0 <= step - 1 < 8:
            full[step - 1] = stage2(w.pop(step - 1))
        if 0 <= step - 2 < 8:
            tail[step - 2] = stage3(step - 2, full.pop(step - 2))
        if 0 <= step - 3 < 8:
            stage4(step - 3, *tail.pop(step - 3))
    sums = dot_nt(wbuf[...], vt[...])
    accv[...] = sums if state_in is None else accv[...] + sums


def make_first(count):
    def first_kernel(*refs):
        attend(refs[:count], refs[count : count + 6], None, refs[count + 6 : count + 10], refs[count + 10 :])

    return first_kernel


def make_next(count):
    def next_kernel(*refs):
        attend(refs[:count], refs[count : count + 6], refs[count + 6 : count + 10], refs[count + 10 : count + 14], refs[count + 14 :])

    return next_kernel


def attend_cost(count):
    return pl.CostEstimate(flops=6_000_000_000 * count, bytes_accessed=4_000_000, transcendentals=1_200_000 * count)


def make_last(count):
    def last_kernel(*refs):
        ops = refs[count : count + 6]
        state_in = refs[count + 6 : count + 10]
        single_ref, fr_ref, frt_ref, wout_ref, gain_ref, wframe_ref, out_ref, frames_ref = refs[
            count + 10 : count + 18
        ]
        m_scr, l_scr, accp, accv, apair, feats = refs[count + 18 : count + 24]
        scr = refs[count + 24 :]
        attend(refs[:count], ops, state_in, (m_scr, l_scr, accp, accv), scr)
        inv = 1.0 / jnp.sum(l_scr[...], axis=1, keepdims=True)
        row = lax.broadcasted_iota(jnp.int32, (256, 128), 0)
        first = jnp.bitwise_and(row, 16) == 0
        col, head = iota((HPAD, 512), 1), iota((HPAD, 512), 0)
        own = jnp.where(col < 192, col >> 4, modulo(col, 96) >> 3)
        vmask = one_where((own == head) & (col < 480))
        attv = jnp.sum((accv[...] * inv).reshape(ROWS, HPAD, 512) * vmask[None], axis=1)
        apair[...] = jnp.where(first, accp[:, 0:128], accp[:, 128:256]) * inv
        feats[:, 0:192] = attv[:, 0:192]
        fr = fr_ref[...]
        rel = [attv[:, 192 + 96 * y : 192 + 96 * (y + 1)] - fr[:, 9 + y : 10 + y] for y in range(3)]
        norm = None
        for x in range(3):
            local = fr[:, x : x + 1] * rel[0] + fr[:, 3 + x : 4 + x] * rel[1] + fr[:, 6 + x : 7 + x] * rel[2]
            norm = local * local if norm is None else norm + local * local
            feats[:, 192 + 96 * x : 192 + 96 * (x + 1)] = local
        feats[:, 480:576] = jnp.sqrt(norm + 1e-08)
        wide = jnp.concatenate([apair[pl.ds(h, ROWS, stride=HPAD), :] for h in range(HEADS)], axis=1).astype(BF16)
        mixed = single_ref[...].astype(F32) + dot(wide, wout_ref[576:2112, :])
        mixed = mixed + dot(feats[...].astype(BF16), wout_ref[0:576, :])
        mean = jnp.mean(mixed, axis=1, keepdims=True)
        center = mixed - mean
        snew = center * lax.rsqrt(jnp.mean(center * center, axis=1, keepdims=True) + 1e-05) * gain_ref[...].reshape(1, CS)
        out_ref[...] = snew.astype(BF16)
        upd = lax.dot_general(
            wframe_ref[...], snew, (((1,), (1,)), ((), ())), preferred_element_type=F32, precision=HI
        )
        ub, uc, ud = upd[0:1, 0:ROWS], upd[1:2, 0:ROWS], upd[2:3, 0:ROWS]
        n = jnp.sqrt(1.0 + ub * ub + uc * uc + ud * ud)
        ua = 1.0 / n
        ub, uc, ud = ub / n, uc / n, ud / n
        ru = [
            [ua * ua + ub * ub - uc * uc - ud * ud, 2.0 * (ub * uc - ua * ud), 2.0 * (ub * ud + ua * uc)],
            [2.0 * (ub * uc + ua * ud), ua * ua - ub * ub + uc * uc - ud * ud, 2.0 * (uc * ud - ua * ub)],
            [2.0 * (ub * ud - ua * uc), 2.0 * (uc * ud + ua * ub), ua * ua - ub * ub - uc * uc + ud * ud],
        ]
        frt = frt_ref[...]
        rot = [[frt[3 * x + y : 3 * x + y + 1] for y in range(3)] for x in range(3)]
        res = []
        for x in range(3):
            for z in range(3):
                res.append(rot[x][0] * ru[0][z] + rot[x][1] * ru[1][z] + rot[x][2] * ru[2][z])
        for x in range(3):
            s = frt[9 + x : 10 + x]
            for y in range(3):
                s = s + rot[x][y] * upd[3 + y : 4 + y, 0:ROWS]
            res.append(s)
        frames_ref[...] = jnp.concatenate(res, axis=0)

    return last_kernel


STRIDE = {"z": 32, "x": 8, "y": 2}
FIRST = (("x", "y"), ("x", "z"))
SECOND = ("z", "y")


def place(d, axis):
    return (d // STRIDE[axis]) % 4


def plane_groups():
    groups = {}
    for d in range(128):
        key = d - (place(d, SECOND[d % 2]) % 2) * STRIDE[SECOND[d % 2]]
        for axis in FIRST[d % 2]:
            key -= place(d, axis) * STRIDE[axis]
        groups.setdefault(key, []).append(d)
    return list(groups.values())


def far_perm():
    perm = []
    for d in range(128):
        at = place(d, SECOND[d % 2])
        perm.append((d, d + (3 - 2 * at) * STRIDE[SECOND[d % 2]]))
    return perm


STATE = ((256, 128), (256, 128), (256, 256), (256, 512))
CORE = [(d, d ^ 1) for d in range(128)]


def attend_scratch(n):
    return [
        pltpu.VMEM((256, n), BF16),
        pltpu.VMEM((256, n), F32),
        pltpu.VMEM((512, n), BF16),
        pltpu.VMEM((K_ALL, n), BF16),
        pltpu.VMEM((256, n), BF16),
    ]


def per_device(
    single, angles, trans, left_factor, right_factor, chain, live,
    w_query, w_keyval, w_qpoints, w_kvpoints, w_pair_in, chain_bias, w_pair_out, w_bias,
    point_weight, w_out, out_gain, w_frame,
):
    vm = pl.BlockSpec(memory_space=pltpu.VMEM)
    packed = pl.pallas_call(
        pack_kernel,
        out_shape=jax.ShapeDtypeStruct((PIECE, PACK), BF16),
        in_specs=[vm] * 6,
        out_specs=vm,
        cost_estimate=pl.CostEstimate(flops=4_000_000_000, bytes_accessed=8_000_000, transcendentals=1000),
    )(single, angles, trans, right_factor, chain[None], live[None])

    own = lax.all_to_all(packed, "blk", 0, 0, tiled=True, axis_index_groups=plane_groups())
    far = lax.ppermute(own, "blk", far_perm())
    near = [own, lax.ppermute(own, "blk", CORE)]

    near[0], single_q = lax.optimization_barrier((own, single))
    *ops, fr, frt = pl.pallas_call(
        query_kernel,
        out_shape=(
            jax.ShapeDtypeStruct((256, K_ALL), BF16),
            jax.ShapeDtypeStruct((2048, 256), BF16),
            jax.ShapeDtypeStruct((320, 256), BF16),
            jax.ShapeDtypeStruct((R_ALL, PACK), BF16),
            jax.ShapeDtypeStruct((16, 128), F32),
            jax.ShapeDtypeStruct((HPAD, 144), BF16),
            jax.ShapeDtypeStruct((ROWS, 128), F32),
            jax.ShapeDtypeStruct((16, ROWS), F32),
        ),
        in_specs=[vm] * 15,
        out_specs=(vm,) * 8,
        scratch_shapes=[pltpu.VMEM((ROWS, K_ALL), F32)],
        compiler_params=pltpu.CompilerParams(vmem_limit_bytes=16 << 20),
        cost_estimate=pl.CostEstimate(flops=600_000_000, bytes_accessed=5_000_000, transcendentals=0),
    )(
        single_q, angles, trans, chain[None], live[None], left_factor, w_query.T, w_qpoints.T, w_pair_in, chain_bias[None], w_pair_out, w_bias.T,
        point_weight[None], w_keyval, w_kvpoints.T,
    )
    scratch = [pltpu.VMEM(shape, F32) for shape in STATE]
    state = pl.pallas_call(
        make_first(len(near)),
        out_shape=tuple(jax.ShapeDtypeStruct(shape, F32) for shape in STATE),
        in_specs=[vm] * (len(near) + len(ops)),
        out_specs=(vm,) * 4,
        scratch_shapes=attend_scratch(PIECE * len(near)),
        compiler_params=pltpu.CompilerParams(vmem_limit_bytes=24 << 20),
        cost_estimate=attend_cost(len(near)),
    )(*near, *ops)
    def further(taken, state):
        return pl.pallas_call(
            make_next(len(taken)),
            out_shape=tuple(jax.ShapeDtypeStruct(shape, F32) for shape in STATE),
            in_specs=[vm] * (len(taken) + len(ops) + 4),
            out_specs=(vm,) * 4,
            scratch_shapes=attend_scratch(PIECE * len(taken)),
            compiler_params=pltpu.CompilerParams(vmem_limit_bytes=20 << 20),
            cost_estimate=attend_cost(len(taken)),
        )(*taken, *ops, *state)

    far, state = lax.optimization_barrier((far, state))
    other = [lax.ppermute(far, "blk", CORE)]
    state = further([far], state)
    out, frames = pl.pallas_call(
        make_last(len(other)),
        out_shape=(
            jax.ShapeDtypeStruct((ROWS, CS), BF16),
            jax.ShapeDtypeStruct((12, ROWS), F32),
        ),
        in_specs=[vm] * (len(other) + len(ops) + 4 + 6),
        out_specs=(vm, vm),
        scratch_shapes=scratch + [pltpu.VMEM((256, 128), F32), pltpu.VMEM((ROWS, 576), F32)] + attend_scratch(PIECE * len(other)),
        compiler_params=pltpu.CompilerParams(vmem_limit_bytes=20 << 20),
        cost_estimate=attend_cost(len(other)),
    )(*other, *ops, *state, single, fr, frt, w_out, out_gain, w_frame.T)
    return out, frames


def solution(mesh):
    in_specs = (
        P("blk", None), P(None, "blk"), P(None, "blk"), P("blk", None), P("blk", None), P("blk"), P("blk"),
    ) + (P(),) * 12
    out_specs = (P("blk", None), P(None, "blk"))
    return jax.shard_map(per_device, mesh=mesh, in_specs=in_specs, out_specs=out_specs, check_vma=False)
```

```python
import math

import jax
import jax.numpy as jnp
from jax import lax
from jax.experimental import pallas as pl
from jax.experimental.pallas import tpu as pltpu
from jax.sharding import PartitionSpec as P

F32 = jnp.float32
BF16 = jnp.bfloat16
HI = lax.Precision.HIGHEST

HEADS, HD, QP, VP, CZ, RANK, CS = 12, 16, 4, 8, 128, 64, 384
ROWS = 16
HPAD = 16
PACK = 512
C_HI, C_MID, C_LO, C_CHAIN, C_LIVE = 64, 76, 88, 100, 108
R_VAL, R_KP, R_VP, R_SEL, R_TILE, R_ALL = 192, 384, 528, 816, 832, 960
K_P = (192, 336, 480)
K_ONE = 624
K_QSQ = 672
K_ALL = 768
C0 = math.sqrt(2.0 / math.pi)
GAMMA = (C0 * 0.044715) ** (1.0 / 3.0)
GB = C0 / GAMMA
S3 = math.sqrt(1.0 / 3.0)
PLANE = 32
PIECE = ROWS * PLANE
COEF = math.sqrt(2.0 / (9.0 * QP)) / 2.0


def dot(a, b):
    return jnp.dot(a, b, preferred_element_type=F32)


def dot_nt(a, b):
    return lax.dot_general(a, b, (((1,), (1,)), ((), ())), preferred_element_type=F32)


def dot_hi(a, b):
    return jnp.dot(a, b, preferred_element_type=F32, precision=HI)


def split3(x):
    hi = x.astype(BF16).astype(F32)
    mid = (x - hi).astype(BF16).astype(F32)
    low = (x - hi - mid).astype(BF16).astype(F32)
    return hi, mid, low


def square_pad(x):
    r, c = x.shape
    if c < 128:
        x = jnp.concatenate([x, jnp.zeros((r, 128 - c), x.dtype)], axis=1)
    if r < 128:
        x = jnp.concatenate([x, jnp.zeros((128 - r, 128), x.dtype)], axis=0)
    return x


def frame_rows(angles_ref, trans_ref, chain_ref, live_ref):
    ang = angles_ref[...]
    cosines, sines = jnp.cos(ang), jnp.sin(ang)
    ca, cb, cc = cosines[0:1], cosines[1:2], cosines[2:3]
    sa, sb, sc = sines[0:1], sines[1:2], sines[2:3]
    rows = [
        ca * cb, -sa * cc + ca * sb * sc, sa * sc + ca * sb * cc,
        sa * cb, ca * cc + sa * sb * sc, -ca * sc + sa * sb * cc,
        -sb, cb * sc, cb * cc,
    ]
    return jnp.concatenate(
        rows
        + [trans_ref[...], chain_ref[...].astype(F32), live_ref[...].astype(F32), jnp.zeros((2, ROWS), F32)],
        axis=0,
    )


def pack_kernel(single_ref, angles_ref, trans_ref, right_ref, chain_ref, live_ref, out_ref):
    wide = square_pad(frame_rows(angles_ref, trans_ref, chain_ref, live_ref)).T[0:ROWS]
    lane = lax.broadcasted_iota(jnp.int32, (ROWS, 128), 1)
    frame = jnp.where(lane < 12, wide, 0.0)
    hi, mid, low = split3(frame)
    tile = pltpu.roll(hi, C_HI, 1) + pltpu.roll(mid, C_MID, 1) + pltpu.roll(low, C_LO, 1)
    chain = wide[:, 12:13]
    live = wide[:, 13:14]
    tile = tile + jnp.where((lane - C_CHAIN).astype(F32) == chain, jnp.where(lane >= C_CHAIN, 1.0, 0.0), 0.0)
    tile = tile + jnp.where(lane == C_LIVE, live, 0.0)
    right = jnp.concatenate([right_ref[...].astype(F32), jnp.zeros((ROWS, 64), F32)], axis=1)
    row = single_ref[...]
    tile = (tile + right).astype(BF16)
    for k in range(PLANE):
        out_ref[ROWS * k : ROWS * (k + 1), 0:CS] = row
        out_ref[ROWS * k : ROWS * (k + 1), CS:PACK] = tile


def iota(shape, axis):
    return lax.broadcasted_iota(jnp.int32, shape, axis)


def modulo(x, m):
    return x - m * jnp.floor((x.astype(F32) + 0.5) * (1.0 / m)).astype(jnp.int32)


def one_where(condition):
    return jnp.where(condition, 1.0, 0.0)


def query_kernel(
    single_ref, angles_ref, trans_ref, chain_ref, live_ref, left_ref, wq_ref, wqp_ref, win_ref, cb_ref, wpo_ref, wb_ref,
    pw_ref, wkv_ref, wkvp_ref, a_ref, wall_ref, cmat_ref, wt_ref, coef_ref, ksum_ref, fr_ref, frt_ref, q_scr,
):
    rows = single_ref[...]
    query = dot_nt(rows, wq_ref[...]).astype(BF16).astype(F32)
    points = dot_nt(rows, wqp_ref[...])
    tall = frame_rows(angles_ref, trans_ref, chain_ref, live_ref)
    frt_ref[...] = tall
    fr = square_pad(tall).T[0:ROWS]
    fr_ref[...] = fr
    pts = [points[:, 48 * y : 48 * (y + 1)] for y in range(3)]
    coef = pw_ref[...] * COEF
    spread = dot_hi(coef, one_where(iota((HEADS, 48), 1) >> 2 == iota((HEADS, 48), 0)))
    q_scr[:, 0:192] = query
    sq = jnp.zeros((ROWS, 48), F32)
    for x in range(3):
        g = fr[:, 9 + x : 10 + x]
        g = g + (fr[:, 3 * x : 3 * x + 1] * pts[0] + fr[:, 3 * x + 1 : 3 * x + 2] * pts[1] + fr[:, 3 * x + 2 : 3 * x + 3] * pts[2])
        sq = sq + g * g
        parts = split3(g * (8.0 * spread))
        for k in range(3):
            q_scr[:, K_P[k] + 48 * x : K_P[k] + 48 * (x + 1)] = parts[k]
    qsq = dot_hi(sq * (-4.0 * spread), one_where(iota((48, HPAD), 0) >> 2 == iota((48, HPAD), 1)))
    q_scr[:, K_ONE:K_QSQ] = jnp.ones((ROWS, 48), F32)
    parts = split3(qsq)
    for k in range(3):
        q_scr[:, K_QSQ + 16 * k : K_QSQ + 16 * (k + 1)] = parts[k]
    q_scr[:, K_QSQ + 48 : K_ALL] = jnp.zeros((ROWS, K_ALL - K_QSQ - 48), F32)
    col, head = iota((HPAD, K_ALL), 1), iota((HPAD, K_ALL), 0)
    of_point = modulo(col, 48) >> 2
    own = jnp.where(col < 192, col >> 4, jnp.where(col < K_ONE, of_point, jnp.bitwise_and(col, 15)))
    mask = one_where((own == head) & (head < HEADS) & (col < K_QSQ + 48))
    for i in range(ROWS):
        a_ref[i * HPAD : (i + 1) * HPAD, :] = (q_scr[i : i + 1, :] * mask).astype(BF16)
    win_t = square_pad(win_ref[...].astype(F32)).T * GAMMA
    cb = cb_ref[...] * GAMMA
    cb_t = square_pad(cb).T[:, 0:1]
    lane = lax.broadcasted_iota(jnp.int32, (128, 128), 1).astype(F32)
    left = left_ref[...].astype(F32)
    left = jnp.concatenate([left, jnp.zeros((ROWS, 64), F32)], axis=1)
    for i in range(ROWS):
        w = win_t * left[i : i + 1, :]
        w = w + jnp.where(lane == fr[i : i + 1, 12:13] + C_CHAIN, cb_t, 0.0)
        hi = w.astype(BF16)
        wall_ref[i * 128 : (i + 1) * 128, 0:128] = hi
        wall_ref[i * 128 : (i + 1) * 128, 128:256] = (w - hi.astype(F32)).astype(BF16)
    w = wpo_ref[...].astype(F32)
    w = (w - jnp.mean(w, axis=1, keepdims=True)) * (0.5 / GAMMA)
    wb_t = jnp.concatenate([wb_ref[...].astype(F32), jnp.zeros((HPAD - HEADS, CZ), F32)], axis=0)
    w_t = w.T
    both = dot_hi(wb_t, w_t)
    hi = both.astype(BF16)
    low = (both - hi.astype(F32)).astype(BF16)
    cmat_ref[...] = jnp.zeros((320, 256), BF16)
    for k in range(2):
        lanes = slice(128 * k, 128 * (k + 1))
        cmat_ref[lanes, lanes] = w_t.astype(BF16)
        cmat_ref[256 + 16 * k : 272 + 16 * k, lanes] = hi
        cmat_ref[288 + 16 * k : 304 + 16 * k, lanes] = low
    wt_ref[0:384, 0:CS] = wkv_ref[...].astype(F32).T.astype(BF16)
    row = iota((432, 432), 0)
    is_key = row < 144
    val = row - 144
    axis = jnp.where(is_key, one_where(row >= 48) + one_where(row >= 96), one_where(val >= 96) + one_where(val >= 192))
    axis = axis.astype(jnp.int32)
    key_at, val_at = row - 48 * axis, val - 96 * axis
    source = jnp.where(
        is_key,
        (key_at >> 2) * (QP + VP) + jnp.bitwise_and(key_at, 3),
        (val_at >> 3) * (QP + VP) + QP + jnp.bitwise_and(val_at, 7),
    )
    perm = one_where(source + 144 * axis == iota((432, 432), 1)).astype(BF16)
    wt_ref[384:816, 0:CS] = dot(perm, wkvp_ref[...]).astype(BF16)
    wt_ref[0:R_ALL, CS:PACK] = jnp.zeros((R_ALL, PACK - CS), BF16)
    wt_ref[R_SEL:R_ALL, 0:CS] = jnp.zeros((R_ALL - R_SEL, CS), BF16)
    row, col = iota((16, 128), 0), iota((16, 128), 1)
    sel = (row < 12) & ((col - row == C_HI) | (col - row == C_MID) | (col - row == C_LO))
    sel = sel | ((row == 12) & (col == C_LIVE))
    wt_ref[R_SEL:R_TILE, CS:PACK] = one_where(sel).astype(BF16)
    wt_ref[R_TILE:R_ALL, CS:PACK] = one_where(iota((128, 128), 0) == iota((128, 128), 1)).astype(BF16)
    ksum_ref[...] = one_where(modulo(iota((HPAD, 144), 1), 48) >> 2 == iota((HPAD, 144), 0)).astype(BF16)
    sub = lax.broadcasted_iota(jnp.int32, (16, HEADS), 0)
    col = lax.broadcasted_iota(jnp.int32, (16, HEADS), 1)
    coef_ref[...] = jnp.broadcast_to(
        jnp.sum(jnp.where(sub == col, -4.0 * coef, 0.0), axis=1, keepdims=True), (16, 128)
    )


def attend(pieces, ops, state_in, state_out, scr):
    a_ref, wall_ref, cmat_ref, wt_ref, coef_ref, ksum_ref = ops
    m_out, l_out, accp, accv = state_out
    wbuf, l0, vt, bmat, wide = scr
    n = PIECE * len(pieces)
    vt[480:512, :] = jnp.zeros((32, n), BF16)
    bmat[K_QSQ:K_ALL, :] = jnp.ones((K_ALL - K_QSQ, n), BF16)
    coef = coef_ref[:, 0:1]
    rows = jnp.concatenate([piece[...] for piece in pieces], axis=0)
    for at in (slice(0, n),):
        kvt = dot_nt(wt_ref[0:R_SEL, 0:CS], rows[:, 0:CS])
        low = dot_nt(wt_ref[R_SEL:R_ALL, CS:PACK], rows[:, CS:PACK])
        tile = low[R_TILE - R_SEL :].astype(BF16)
        wide[0:128, at] = tile
        wide[128:256, at] = tile
        bmat[0:192, at] = kvt[0:192].astype(BF16)
        vt[0:192, at] = kvt[R_VAL : R_VAL + 192].astype(BF16)
        sel = low[0:16]
        ksq = None
        for x in range(3):
            r = [sel[3 * x + y : 3 * x + y + 1] for y in range(3)]
            t = sel[9 + x : 10 + x]
            kp = t
            vp = t
            for y in range(3):
                kp = kp + r[y] * kvt[R_KP + 48 * y : R_KP + 48 * (y + 1)]
                vp = vp + r[y] * kvt[R_VP + 96 * y : R_VP + 96 * (y + 1)]
            kb = kp.astype(BF16)
            for k in range(3):
                bmat[K_P[k] + 48 * x : K_P[k] + 48 * (x + 1), at] = kb
            vt[192 + 96 * x : 192 + 96 * (x + 1), at] = vp.astype(BF16)
            kf = kb.astype(F32)
            ksq = kf * kf if ksq is None else ksq + kf * kf
        hi, mid, lo = split3(ksq)
        ks = dot(ksum_ref[...], jnp.concatenate([hi, mid, lo], axis=0).astype(BF16))
        dead = 100000.0 * (1.0 - sel[12:13])
        ks = ks * coef - (4.0 / S3) * dead
        hi, mid, lo = split3(ks)
        bmat[K_ONE : K_ONE + 48, at] = jnp.concatenate([hi, mid, lo], axis=0).astype(BF16)
    l0[...] = dot(a_ref[...], bmat[...]) * (S3 / 4.0)

    def stage1(p):
        return dot(wall_ref[p * 256 : (p + 1) * 256, :], wide[...])

    def stage2(w):
        t = jnp.tanh(w * (w * w + GB))
        hid = (w + w * t).astype(BF16)
        return dot(cmat_ref[...], hid)

    def stage3(p, full):
        at = slice(p * 32, (p + 1) * 32)
        center = full[0:256]
        cb = center.astype(BF16)
        sq = center * center
        rs = []
        for k in range(2):
            var = jnp.sum(sq[128 * k : 128 * (k + 1)], axis=0, keepdims=True) * (1.0 / CZ)
            rs.append(jnp.broadcast_to(lax.rsqrt(var + 1e-05), (16, n)))
        rs = jnp.concatenate(rs, axis=0)
        logits = l0[at, :] + (full[256:288] + full[288:320]) * (rs * S3)
        new = jnp.max(logits, axis=1, keepdims=True)
        factor = None
        if state_in is not None:
            top = state_in[0][at, :]
            new = jnp.maximum(top, new)
            factor = jnp.exp(top - new)
        terms = jnp.exp(logits - new[:, 0:1])
        m_out[at, :] = jnp.broadcast_to(new, (32, 128))
        part = terms[:, 0:128]
        for k in range(1, n // 128):
            part = part + terms[:, 128 * k : 128 * (k + 1)]
        wbuf[at, :] = terms.astype(BF16)
        return cb, (terms * rs).astype(BF16), part, factor

    def stage4(p, cb, wr, part, factor):
        at = slice(p * 32, (p + 1) * 32)
        pair_sum = dot_nt(wr, cb)
        if state_in is not None:
            part = part + state_in[1][at, :] * factor
            f2 = jnp.concatenate([factor, factor], axis=1)
            pair_sum = pair_sum + state_in[2][at, :] * f2
            accv[at, :] = state_in[3][at, :] * jnp.concatenate([f2, f2], axis=1)
        l_out[at, :] = part
        accp[at, :] = pair_sum

    w, full, tail = {}, {}, {}
    for step in range(8 + 3):
        if step < 8:
            w[step] = stage1(step)
        if 0 <= step - 1 < 8:
            full[step - 1] = stage2(w.pop(step - 1))
        if 0 <= step - 2 < 8:
            tail[step - 2] = stage3(step - 2, full.pop(step - 2))
        if step - 2 == 7:
            sums = dot_nt(wbuf[...], vt[...])
        if 0 <= step - 3 < 8:
            stage4(step - 3, *tail.pop(step - 3))
    accv[...] = sums if state_in is None else accv[...] + sums


def make_first(count):
    def first_kernel(*refs):
        attend(refs[:count], refs[count : count + 6], None, refs[count + 6 : count + 10], refs[count + 10 :])

    return first_kernel


def make_next(count):
    def next_kernel(*refs):
        attend(refs[:count], refs[count : count + 6], refs[count + 6 : count + 10], refs[count + 10 : count + 14], refs[count + 14 :])

    return next_kernel


def attend_cost(count):
    return pl.CostEstimate(flops=6_000_000_000 * count, bytes_accessed=4_000_000, transcendentals=1_200_000 * count)


def make_last(count):
    def last_kernel(*refs):
        ops = refs[count : count + 6]
        state_in = refs[count + 6 : count + 10]
        single_ref, fr_ref, frt_ref, wout_ref, gain_ref, wframe_ref, out_ref, frames_ref = refs[
            count + 10 : count + 18
        ]
        m_scr, l_scr, accp, accv, apair, feats = refs[count + 18 : count + 24]
        scr = refs[count + 24 :]
        attend(refs[:count], ops, state_in, (m_scr, l_scr, accp, accv), scr)
        inv = 1.0 / jnp.sum(l_scr[...], axis=1, keepdims=True)
        row = lax.broadcasted_iota(jnp.int32, (256, 128), 0)
        first = jnp.bitwise_and(row, 16) == 0
        col, head = iota((HPAD, 512), 1), iota((HPAD, 512), 0)
        own = jnp.where(col < 192, col >> 4, modulo(col, 96) >> 3)
        vmask = one_where((own == head) & (col < 480))
        attv = jnp.sum((accv[...] * inv).reshape(ROWS, HPAD, 512) * vmask[None], axis=1)
        apair[...] = jnp.where(first, accp[:, 0:128], accp[:, 128:256]) * inv
        feats[:, 0:192] = attv[:, 0:192]
        fr = fr_ref[...]
        rel = [attv[:, 192 + 96 * y : 192 + 96 * (y + 1)] - fr[:, 9 + y : 10 + y] for y in range(3)]
        norm = None
        for x in range(3):
            local = fr[:, x : x + 1] * rel[0] + fr[:, 3 + x : 4 + x] * rel[1] + fr[:, 6 + x : 7 + x] * rel[2]
            norm = local * local if norm is None else norm + local * local
            feats[:, 192 + 96 * x : 192 + 96 * (x + 1)] = local
        feats[:, 480:576] = jnp.sqrt(norm + 1e-08)
        wide = jnp.concatenate([apair[pl.ds(h, ROWS, stride=HPAD), :] for h in range(HEADS)], axis=1).astype(BF16)
        mixed = single_ref[...].astype(F32) + dot(wide, wout_ref[576:2112, :])
        mixed = mixed + dot(feats[...].astype(BF16), wout_ref[0:576, :])
        mean = jnp.mean(mixed, axis=1, keepdims=True)
        center = mixed - mean
        snew = center * lax.rsqrt(jnp.mean(center * center, axis=1, keepdims=True) + 1e-05) * gain_ref[...].reshape(1, CS)
        out_ref[...] = snew.astype(BF16)
        upd = lax.dot_general(
            wframe_ref[...], snew, (((1,), (1,)), ((), ())), preferred_element_type=F32, precision=HI
        )
        ub, uc, ud = upd[0:1, 0:ROWS], upd[1:2, 0:ROWS], upd[2:3, 0:ROWS]
        n = jnp.sqrt(1.0 + ub * ub + uc * uc + ud * ud)
        ua = 1.0 / n
        ub, uc, ud = ub / n, uc / n, ud / n
        ru = [
            [ua * ua + ub * ub - uc * uc - ud * ud, 2.0 * (ub * uc - ua * ud), 2.0 * (ub * ud + ua * uc)],
            [2.0 * (ub * uc + ua * ud), ua * ua - ub * ub + uc * uc - ud * ud, 2.0 * (uc * ud - ua * ub)],
            [2.0 * (ub * ud - ua * uc), 2.0 * (uc * ud + ua * ub), ua * ua - ub * ub - uc * uc + ud * ud],
        ]
        frt = frt_ref[...]
        rot = [[frt[3 * x + y : 3 * x + y + 1] for y in range(3)] for x in range(3)]
        res = []
        for x in range(3):
            for z in range(3):
                res.append(rot[x][0] * ru[0][z] + rot[x][1] * ru[1][z] + rot[x][2] * ru[2][z])
        for x in range(3):
            s = frt[9 + x : 10 + x]
            for y in range(3):
                s = s + rot[x][y] * upd[3 + y : 4 + y, 0:ROWS]
            res.append(s)
        frames_ref[...] = jnp.concatenate(res, axis=0)

    return last_kernel


STRIDE = {"z": 32, "x": 8, "y": 2}
FIRST = (("x", "y"), ("x", "z"))
SECOND = ("z", "y")


def place(d, axis):
    return (d // STRIDE[axis]) % 4


def plane_groups():
    groups = {}
    for d in range(128):
        key = d - (place(d, SECOND[d % 2]) % 2) * STRIDE[SECOND[d % 2]]
        for axis in FIRST[d % 2]:
            key -= place(d, axis) * STRIDE[axis]
        groups.setdefault(key, []).append(d)
    return list(groups.values())


def far_perm():
    perm = []
    for d in range(128):
        at = place(d, SECOND[d % 2])
        perm.append((d, d + (3 - 2 * at) * STRIDE[SECOND[d % 2]]))
    return perm


STATE = ((256, 128), (256, 128), (256, 256), (256, 512))
CORE = [(d, d ^ 1) for d in range(128)]


def attend_scratch(n):
    return [
        pltpu.VMEM((256, n), BF16),
        pltpu.VMEM((256, n), F32),
        pltpu.VMEM((512, n), BF16),
        pltpu.VMEM((K_ALL, n), BF16),
        pltpu.VMEM((256, n), BF16),
    ]


def per_device(
    single, angles, trans, left_factor, right_factor, chain, live,
    w_query, w_keyval, w_qpoints, w_kvpoints, w_pair_in, chain_bias, w_pair_out, w_bias,
    point_weight, w_out, out_gain, w_frame,
):
    vm = pl.BlockSpec(memory_space=pltpu.VMEM)
    packed = pl.pallas_call(
        pack_kernel,
        out_shape=jax.ShapeDtypeStruct((PIECE, PACK), BF16),
        in_specs=[vm] * 6,
        out_specs=vm,
        cost_estimate=pl.CostEstimate(flops=4_000_000_000, bytes_accessed=8_000_000, transcendentals=1000),
    )(single, angles, trans, right_factor, chain[None], live[None])

    own = lax.all_to_all(packed, "blk", 0, 0, tiled=True, axis_index_groups=plane_groups())
    far = lax.ppermute(own, "blk", far_perm())
    near = [own, lax.ppermute(own, "blk", CORE)]

    near[0], single_q = lax.optimization_barrier((own, single))
    *ops, fr, frt = pl.pallas_call(
        query_kernel,
        out_shape=(
            jax.ShapeDtypeStruct((256, K_ALL), BF16),
            jax.ShapeDtypeStruct((2048, 256), BF16),
            jax.ShapeDtypeStruct((320, 256), BF16),
            jax.ShapeDtypeStruct((R_ALL, PACK), BF16),
            jax.ShapeDtypeStruct((16, 128), F32),
            jax.ShapeDtypeStruct((HPAD, 144), BF16),
            jax.ShapeDtypeStruct((ROWS, 128), F32),
            jax.ShapeDtypeStruct((16, ROWS), F32),
        ),
        in_specs=[vm] * 15,
        out_specs=(vm,) * 8,
        scratch_shapes=[pltpu.VMEM((ROWS, K_ALL), F32)],
        compiler_params=pltpu.CompilerParams(vmem_limit_bytes=16 << 20),
        cost_estimate=pl.CostEstimate(flops=600_000_000, bytes_accessed=5_000_000, transcendentals=0),
    )(
        single_q, angles, trans, chain[None], live[None], left_factor, w_query.T, w_qpoints.T, w_pair_in, chain_bias[None], w_pair_out, w_bias.T,
        point_weight[None], w_keyval, w_kvpoints.T,
    )
    scratch = [pltpu.VMEM(shape, F32) for shape in STATE]
    state = pl.pallas_call(
        make_first(len(near)),
        out_shape=tuple(jax.ShapeDtypeStruct(shape, F32) for shape in STATE),
        in_specs=[vm] * (len(near) + len(ops)),
        out_specs=(vm,) * 4,
        scratch_shapes=attend_scratch(PIECE * len(near)),
        compiler_params=pltpu.CompilerParams(vmem_limit_bytes=24 << 20),
        cost_estimate=attend_cost(len(near)),
    )(*near, *ops)
    def further(taken, state):
        return pl.pallas_call(
            make_next(len(taken)),
            out_shape=tuple(jax.ShapeDtypeStruct(shape, F32) for shape in STATE),
            in_specs=[vm] * (len(taken) + len(ops) + 4),
            out_specs=(vm,) * 4,
            scratch_shapes=attend_scratch(PIECE * len(taken)),
            compiler_params=pltpu.CompilerParams(vmem_limit_bytes=20 << 20),
            cost_estimate=attend_cost(len(taken)),
        )(*taken, *ops, *state)

    far, state = lax.optimization_barrier((far, state))
    other = [lax.ppermute(far, "blk", CORE)]
    state = further([far], state)
    out, frames = pl.pallas_call(
        make_last(len(other)),
        out_shape=(
            jax.ShapeDtypeStruct((ROWS, CS), BF16),
            jax.ShapeDtypeStruct((12, ROWS), F32),
        ),
        in_specs=[vm] * (len(other) + len(ops) + 4 + 6),
        out_specs=(vm, vm),
        scratch_shapes=scratch + [pltpu.VMEM((256, 128), F32), pltpu.VMEM((ROWS, 576), F32)] + attend_scratch(PIECE * len(other)),
        compiler_params=pltpu.CompilerParams(vmem_limit_bytes=20 << 20),
        cost_estimate=attend_cost(len(other)),
    )(*other, *ops, *state, single, fr, frt, w_out, out_gain, w_frame.T)
    return out, frames


def solution(mesh):
    in_specs = (
        P("blk", None), P(None, "blk"), P(None, "blk"), P("blk", None), P("blk", None), P("blk"), P("blk"),
    ) + (P(),) * 12
    out_specs = (P("blk", None), P(None, "blk"))
    return jax.shard_map(per_device, mesh=mesh, in_specs=in_specs, out_specs=out_specs, check_vma=False)
```

```python
import math

import jax
import jax.numpy as jnp
from jax import lax
from jax.experimental import pallas as pl
from jax.experimental.pallas import tpu as pltpu
from jax.sharding import PartitionSpec as P

F32 = jnp.float32
BF16 = jnp.bfloat16
HI = lax.Precision.HIGHEST

HEADS, HD, QP, VP, CZ, RANK, CS = 12, 16, 4, 8, 128, 64, 384
ROWS = 16
HPAD = 16
PACK = 512
C_HI, C_MID, C_LO, C_CHAIN, C_LIVE = 64, 76, 88, 100, 108
R_VAL, R_KP, R_VP, R_SEL, R_TILE, R_ALL = 192, 384, 528, 816, 832, 960
K_P = (192, 336, 480)
K_ONE = 624
K_QSQ = 672
K_ALL = 768
C0 = math.sqrt(2.0 / math.pi)
GAMMA = (C0 * 0.044715) ** (1.0 / 3.0)
GB = C0 / GAMMA
S3 = math.sqrt(1.0 / 3.0)
PLANE = 32
PIECE = ROWS * PLANE
COEF = math.sqrt(2.0 / (9.0 * QP)) / 2.0


def dot(a, b):
    return jnp.dot(a, b, preferred_element_type=F32)


def dot_nt(a, b):
    return lax.dot_general(a, b, (((1,), (1,)), ((), ())), preferred_element_type=F32)


def dot_hi(a, b):
    return jnp.dot(a, b, preferred_element_type=F32, precision=HI)


def split3(x):
    hi = x.astype(BF16).astype(F32)
    mid = (x - hi).astype(BF16).astype(F32)
    low = (x - hi - mid).astype(BF16).astype(F32)
    return hi, mid, low


def square_pad(x):
    r, c = x.shape
    if c < 128:
        x = jnp.concatenate([x, jnp.zeros((r, 128 - c), x.dtype)], axis=1)
    if r < 128:
        x = jnp.concatenate([x, jnp.zeros((128 - r, 128), x.dtype)], axis=0)
    return x


def frame_rows(angles_ref, trans_ref, chain_ref, live_ref):
    ang = angles_ref[...]
    cosines, sines = jnp.cos(ang), jnp.sin(ang)
    ca, cb, cc = cosines[0:1], cosines[1:2], cosines[2:3]
    sa, sb, sc = sines[0:1], sines[1:2], sines[2:3]
    rows = [
        ca * cb, -sa * cc + ca * sb * sc, sa * sc + ca * sb * cc,
        sa * cb, ca * cc + sa * sb * sc, -ca * sc + sa * sb * cc,
        -sb, cb * sc, cb * cc,
    ]
    return jnp.concatenate(
        rows
        + [trans_ref[...], chain_ref[...].astype(F32), live_ref[...].astype(F32), jnp.zeros((2, ROWS), F32)],
        axis=0,
    )


def pack_kernel(single_ref, angles_ref, trans_ref, right_ref, chain_ref, live_ref, out_ref):
    wide = square_pad(frame_rows(angles_ref, trans_ref, chain_ref, live_ref)).T[0:ROWS]
    lane = lax.broadcasted_iota(jnp.int32, (ROWS, 128), 1)
    frame = jnp.where(lane < 12, wide, 0.0)
    hi, mid, low = split3(frame)
    tile = pltpu.roll(hi, C_HI, 1) + pltpu.roll(mid, C_MID, 1) + pltpu.roll(low, C_LO, 1)
    chain = wide[:, 12:13]
    live = wide[:, 13:14]
    tile = tile + jnp.where((lane - C_CHAIN).astype(F32) == chain, jnp.where(lane >= C_CHAIN, 1.0, 0.0), 0.0)
    tile = tile + jnp.where(lane == C_LIVE, live, 0.0)
    right = jnp.concatenate([right_ref[...].astype(F32), jnp.zeros((ROWS, 64), F32)], axis=1)
    row = single_ref[...]
    tile = (tile + right).astype(BF16)
    for k in range(PLANE):
        out_ref[ROWS * k : ROWS * (k + 1), 0:CS] = row
        out_ref[ROWS * k : ROWS * (k + 1), CS:PACK] = tile


def iota(shape, axis):
    return lax.broadcasted_iota(jnp.int32, shape, axis)


def modulo(x, m):
    return x - m * jnp.floor((x.astype(F32) + 0.5) * (1.0 / m)).astype(jnp.int32)


def one_where(condition):
    return jnp.where(condition, 1.0, 0.0)


def query_kernel(
    single_ref, angles_ref, trans_ref, chain_ref, live_ref, left_ref, wq_ref, wqp_ref, win_ref, cb_ref, wpo_ref, wb_ref,
    pw_ref, wkv_ref, wkvp_ref, a_ref, wall_ref, cmat_ref, wt_ref, coef_ref, ksum_ref, fr_ref, frt_ref, q_scr,
):
    rows = single_ref[...]
    query = dot_nt(rows, wq_ref[...]).astype(BF16).astype(F32)
    points = dot_nt(rows, wqp_ref[...])
    tall = frame_rows(angles_ref, trans_ref, chain_ref, live_ref)
    frt_ref[...] = tall
    fr = square_pad(tall).T[0:ROWS]
    fr_ref[...] = fr
    pts = [points[:, 48 * y : 48 * (y + 1)] for y in range(3)]
    coef = pw_ref[...] * COEF
    spread = dot_hi(coef, one_where(iota((HEADS, 48), 1) >> 2 == iota((HEADS, 48), 0)))
    q_scr[:, 0:192] = query
    sq = jnp.zeros((ROWS, 48), F32)
    for x in range(3):
        g = fr[:, 9 + x : 10 + x]
        g = g + (fr[:, 3 * x : 3 * x + 1] * pts[0] + fr[:, 3 * x + 1 : 3 * x + 2] * pts[1] + fr[:, 3 * x + 2 : 3 * x + 3] * pts[2])
        sq = sq + g * g
        parts = split3(g * (8.0 * spread))
        for k in range(3):
            q_scr[:, K_P[k] + 48 * x : K_P[k] + 48 * (x + 1)] = parts[k]
    qsq = dot_hi(sq * (-4.0 * spread), one_where(iota((48, HPAD), 0) >> 2 == iota((48, HPAD), 1)))
    q_scr[:, K_ONE:K_QSQ] = jnp.ones((ROWS, 48), F32)
    parts = split3(qsq)
    for k in range(3):
        q_scr[:, K_QSQ + 16 * k : K_QSQ + 16 * (k + 1)] = parts[k]
    q_scr[:, K_QSQ + 48 : K_ALL] = jnp.zeros((ROWS, K_ALL - K_QSQ - 48), F32)
    col, head = iota((HPAD, K_ALL), 1), iota((HPAD, K_ALL), 0)
    of_point = modulo(col, 48) >> 2
    own = jnp.where(col < 192, col >> 4, jnp.where(col < K_ONE, of_point, jnp.bitwise_and(col, 15)))
    mask = one_where((own == head) & (head < HEADS) & (col < K_QSQ + 48))
    for i in range(ROWS):
        a_ref[i * HPAD : (i + 1) * HPAD, :] = (q_scr[i : i + 1, :] * mask).astype(BF16)
    win_t = square_pad(win_ref[...].astype(F32)).T * GAMMA
    cb = cb_ref[...] * GAMMA
    cb_t = square_pad(cb).T[:, 0:1]
    lane = lax.broadcasted_iota(jnp.int32, (128, 128), 1).astype(F32)
    left = left_ref[...].astype(F32)
    left = jnp.concatenate([left, jnp.zeros((ROWS, 64), F32)], axis=1)
    for i in range(ROWS):
        w = win_t * left[i : i + 1, :]
        w = w + jnp.where(lane == fr[i : i + 1, 12:13] + C_CHAIN, cb_t, 0.0)
        hi = w.astype(BF16)
        wall_ref[i * 128 : (i + 1) * 128, 0:128] = hi
        wall_ref[i * 128 : (i + 1) * 128, 128:256] = (w - hi.astype(F32)).astype(BF16)
    w = wpo_ref[...].astype(F32)
    w = (w - jnp.mean(w, axis=1, keepdims=True)) * (0.5 / GAMMA)
    wb_t = jnp.concatenate([wb_ref[...].astype(F32), jnp.zeros((HPAD - HEADS, CZ), F32)], axis=0)
    w_t = w.T
    both = dot_hi(wb_t, w_t)
    hi = both.astype(BF16)
    low = (both - hi.astype(F32)).astype(BF16)
    cmat_ref[...] = jnp.zeros((320, 256), BF16)
    for k in range(2):
        lanes = slice(128 * k, 128 * (k + 1))
        cmat_ref[lanes, lanes] = w_t.astype(BF16)
        cmat_ref[256 + 16 * k : 272 + 16 * k, lanes] = hi
        cmat_ref[288 + 16 * k : 304 + 16 * k, lanes] = low
    wt_ref[0:384, 0:CS] = wkv_ref[...].astype(F32).T.astype(BF16)
    row = iota((432, 432), 0)
    is_key = row < 144
    val = row - 144
    axis = jnp.where(is_key, one_where(row >= 48) + one_where(row >= 96), one_where(val >= 96) + one_where(val >= 192))
    axis = axis.astype(jnp.int32)
    key_at, val_at = row - 48 * axis, val - 96 * axis
    source = jnp.where(
        is_key,
        (key_at >> 2) * (QP + VP) + jnp.bitwise_and(key_at, 3),
        (val_at >> 3) * (QP + VP) + QP + jnp.bitwise_and(val_at, 7),
    )
    perm = one_where(source + 144 * axis == iota((432, 432), 1)).astype(BF16)
    wt_ref[384:816, 0:CS] = dot(perm, wkvp_ref[...]).astype(BF16)
    wt_ref[0:R_ALL, CS:PACK] = jnp.zeros((R_ALL, PACK - CS), BF16)
    wt_ref[R_SEL:R_ALL, 0:CS] = jnp.zeros((R_ALL - R_SEL, CS), BF16)
    row, col = iota((16, 128), 0), iota((16, 128), 1)
    sel = (row < 12) & ((col - row == C_HI) | (col - row == C_MID) | (col - row == C_LO))
    sel = sel | ((row == 12) & (col == C_LIVE))
    wt_ref[R_SEL:R_TILE, CS:PACK] = one_where(sel).astype(BF16)
    wt_ref[R_TILE:R_ALL, CS:PACK] = one_where(iota((128, 128), 0) == iota((128, 128), 1)).astype(BF16)
    ksum_ref[...] = one_where(modulo(iota((HPAD, 144), 1), 48) >> 2 == iota((HPAD, 144), 0)).astype(BF16)
    sub = lax.broadcasted_iota(jnp.int32, (16, HEADS), 0)
    col = lax.broadcasted_iota(jnp.int32, (16, HEADS), 1)
    coef_ref[...] = jnp.broadcast_to(
        jnp.sum(jnp.where(sub == col, -4.0 * coef, 0.0), axis=1, keepdims=True), (16, 128)
    )


def attend(pieces, ops, state_in, state_out, scr):
    a_ref, wall_ref, cmat_ref, wt_ref, coef_ref, ksum_ref = ops
    m_out, l_out, accp, accv = state_out
    wbuf, l0, vt, bmat, wide = scr
    n = PIECE * len(pieces)
    vt[480:512, :] = jnp.zeros((32, n), BF16)
    bmat[K_QSQ:K_ALL, :] = jnp.ones((K_ALL - K_QSQ, n), BF16)
    coef = coef_ref[:, 0:1]
    rows = jnp.concatenate([piece[...] for piece in pieces], axis=0)
    for at in (slice(0, n),):
        kvt = dot_nt(wt_ref[0:R_SEL, 0:CS], rows[:, 0:CS])
        low = dot_nt(wt_ref[R_SEL:R_ALL, CS:PACK], rows[:, CS:PACK])
        tile = low[R_TILE - R_SEL :].astype(BF16)
        wide[0:128, at] = tile
        wide[128:256, at] = tile
        bmat[0:192, at] = kvt[0:192].astype(BF16)
        vt[0:192, at] = kvt[R_VAL : R_VAL + 192].astype(BF16)
        sel = low[0:16]
        ksq = None
        for x in range(3):
            r = [sel[3 * x + y : 3 * x + y + 1] for y in range(3)]
            t = sel[9 + x : 10 + x]
            kp = t
            vp = t
            for y in range(3):
                kp = kp + r[y] * kvt[R_KP + 48 * y : R_KP + 48 * (y + 1)]
                vp = vp + r[y] * kvt[R_VP + 96 * y : R_VP + 96 * (y + 1)]
            kb = kp.astype(BF16)
            for k in range(3):
                bmat[K_P[k] + 48 * x : K_P[k] + 48 * (x + 1), at] = kb
            vt[192 + 96 * x : 192 + 96 * (x + 1), at] = vp.astype(BF16)
            kf = kb.astype(F32)
            ksq = kf * kf if ksq is None else ksq + kf * kf
        hi, mid, lo = split3(ksq)
        ks = dot(ksum_ref[...], jnp.concatenate([hi, mid, lo], axis=0).astype(BF16))
        dead = 100000.0 * (1.0 - sel[12:13])
        ks = ks * coef - (4.0 / S3) * dead
        hi, mid, lo = split3(ks)
        bmat[K_ONE : K_ONE + 48, at] = jnp.concatenate([hi, mid, lo], axis=0).astype(BF16)
    l0[...] = dot(a_ref[...], bmat[...]) * (S3 / 4.0)

    def stage1(p):
        return dot(wall_ref[p * 256 : (p + 1) * 256, :], wide[...])

    def stage2(w):
        t = jnp.tanh(w * (w * w + GB))
        hid = (w + w * t).astype(BF16)
        return dot(cmat_ref[...], hid)

    def stage3(p, full):
        at = slice(p * 32, (p + 1) * 32)
        center = full[0:256]
        cb = center.astype(BF16)
        sq = center * center
        rs = []
        for k in range(2):
            var = jnp.sum(sq[128 * k : 128 * (k + 1)], axis=0, keepdims=True) * (1.0 / CZ)
            rs.append(jnp.broadcast_to(lax.rsqrt(var + 1e-05), (16, n)))
        rs = jnp.concatenate(rs, axis=0)
        logits = l0[at, :] + (full[256:288] + full[288:320]) * (rs * S3)
        new = jnp.max(logits, axis=1, keepdims=True)
        factor = None
        if state_in is not None:
            top = state_in[0][at, :]
            new = jnp.maximum(top, new)
            factor = jnp.exp(top - new)
        terms = jnp.exp(logits - new[:, 0:1])
        m_out[at, :] = jnp.broadcast_to(new, (32, 128))
        part = terms[:, 0:128]
        for k in range(1, n // 128):
            part = part + terms[:, 128 * k : 128 * (k + 1)]
        wbuf[at, :] = terms.astype(BF16)
        return cb, (terms * rs).astype(BF16), part, factor

    def stage4(p, cb, wr, part, factor):
        at = slice(p * 32, (p + 1) * 32)
        pair_sum = dot_nt(wr, cb)
        if state_in is not None:
            part = part + state_in[1][at, :] * factor
            f2 = jnp.concatenate([factor, factor], axis=1)
            pair_sum = pair_sum + state_in[2][at, :] * f2
            accv[at, :] = state_in[3][at, :] * jnp.concatenate([f2, f2], axis=1)
        l_out[at, :] = part
        accp[at, :] = pair_sum

    w, full, tail = {}, {}, {}
    for step in range(8 + 3):
        if step < 8:
            w[step] = stage1(step)
        if 0 <= step - 2 < 8:
            tail[step - 2] = stage3(step - 2, full.pop(step - 2))
        if 0 <= step - 1 < 8:
            full[step - 1] = stage2(w.pop(step - 1))
        if step - 2 == 7:
            sums = dot_nt(wbuf[...], vt[...])
        if 0 <= step - 3 < 8:
            stage4(step - 3, *tail.pop(step - 3))
    accv[...] = sums if state_in is None else accv[...] + sums


def make_first(count):
    def first_kernel(*refs):
        attend(refs[:count], refs[count : count + 6], None, refs[count + 6 : count + 10], refs[count + 10 :])

    return first_kernel


def make_next(count):
    def next_kernel(*refs):
        attend(refs[:count], refs[count : count + 6], refs[count + 6 : count + 10], refs[count + 10 : count + 14], refs[count + 14 :])

    return next_kernel


def attend_cost(count):
    return pl.CostEstimate(flops=6_000_000_000 * count, bytes_accessed=4_000_000, transcendentals=1_200_000 * count)


def make_last(count):
    def last_kernel(*refs):
        ops = refs[count : count + 6]
        state_in = refs[count + 6 : count + 10]
        single_ref, fr_ref, frt_ref, wout_ref, gain_ref, wframe_ref, out_ref, frames_ref = refs[
            count + 10 : count + 18
        ]
        m_scr, l_scr, accp, accv, apair, feats = refs[count + 18 : count + 24]
        scr = refs[count + 24 :]
        attend(refs[:count], ops, state_in, (m_scr, l_scr, accp, accv), scr)
        inv = 1.0 / jnp.sum(l_scr[...], axis=1, keepdims=True)
        row = lax.broadcasted_iota(jnp.int32, (256, 128), 0)
        first = jnp.bitwise_and(row, 16) == 0
        col, head = iota((HPAD, 512), 1), iota((HPAD, 512), 0)
        own = jnp.where(col < 192, col >> 4, modulo(col, 96) >> 3)
        vmask = one_where((own == head) & (col < 480))
        attv = jnp.sum((accv[...] * inv).reshape(ROWS, HPAD, 512) * vmask[None], axis=1)
        apair[...] = jnp.where(first, accp[:, 0:128], accp[:, 128:256]) * inv
        feats[:, 0:192] = attv[:, 0:192]
        fr = fr_ref[...]
        rel = [attv[:, 192 + 96 * y : 192 + 96 * (y + 1)] - fr[:, 9 + y : 10 + y] for y in range(3)]
        norm = None
        for x in range(3):
            local = fr[:, x : x + 1] * rel[0] + fr[:, 3 + x : 4 + x] * rel[1] + fr[:, 6 + x : 7 + x] * rel[2]
            norm = local * local if norm is None else norm + local * local
            feats[:, 192 + 96 * x : 192 + 96 * (x + 1)] = local
        feats[:, 480:576] = jnp.sqrt(norm + 1e-08)
        wide = jnp.concatenate([apair[pl.ds(h, ROWS, stride=HPAD), :] for h in range(HEADS)], axis=1).astype(BF16)
        mixed = single_ref[...].astype(F32) + dot(wide, wout_ref[576:2112, :])
        mixed = mixed + dot(feats[...].astype(BF16), wout_ref[0:576, :])
        mean = jnp.mean(mixed, axis=1, keepdims=True)
        center = mixed - mean
        snew = center * lax.rsqrt(jnp.mean(center * center, axis=1, keepdims=True) + 1e-05) * gain_ref[...].reshape(1, CS)
        out_ref[...] = snew.astype(BF16)
        upd = lax.dot_general(
            wframe_ref[...], snew, (((1,), (1,)), ((), ())), preferred_element_type=F32, precision=HI
        )
        ub, uc, ud = upd[0:1, 0:ROWS], upd[1:2, 0:ROWS], upd[2:3, 0:ROWS]
        n = jnp.sqrt(1.0 + ub * ub + uc * uc + ud * ud)
        ua = 1.0 / n
        ub, uc, ud = ub / n, uc / n, ud / n
        ru = [
            [ua * ua + ub * ub - uc * uc - ud * ud, 2.0 * (ub * uc - ua * ud), 2.0 * (ub * ud + ua * uc)],
            [2.0 * (ub * uc + ua * ud), ua * ua - ub * ub + uc * uc - ud * ud, 2.0 * (uc * ud - ua * ub)],
            [2.0 * (ub * ud - ua * uc), 2.0 * (uc * ud + ua * ub), ua * ua - ub * ub - uc * uc + ud * ud],
        ]
        frt = frt_ref[...]
        rot = [[frt[3 * x + y : 3 * x + y + 1] for y in range(3)] for x in range(3)]
        res = []
        for x in range(3):
            for z in range(3):
                res.append(rot[x][0] * ru[0][z] + rot[x][1] * ru[1][z] + rot[x][2] * ru[2][z])
        for x in range(3):
            s = frt[9 + x : 10 + x]
            for y in range(3):
                s = s + rot[x][y] * upd[3 + y : 4 + y, 0:ROWS]
            res.append(s)
        frames_ref[...] = jnp.concatenate(res, axis=0)

    return last_kernel


STRIDE = {"z": 32, "x": 8, "y": 2}
FIRST = (("x", "y"), ("x", "z"))
SECOND = ("z", "y")


def place(d, axis):
    return (d // STRIDE[axis]) % 4


def plane_groups():
    groups = {}
    for d in range(128):
        key = d - (place(d, SECOND[d % 2]) % 2) * STRIDE[SECOND[d % 2]]
        for axis in FIRST[d % 2]:
            key -= place(d, axis) * STRIDE[axis]
        groups.setdefault(key, []).append(d)
    return list(groups.values())


def far_perm():
    perm = []
    for d in range(128):
        at = place(d, SECOND[d % 2])
        perm.append((d, d + (3 - 2 * at) * STRIDE[SECOND[d % 2]]))
    return perm


STATE = ((256, 128), (256, 128), (256, 256), (256, 512))
CORE = [(d, d ^ 1) for d in range(128)]


def attend_scratch(n):
    return [
        pltpu.VMEM((256, n), BF16),
        pltpu.VMEM((256, n), F32),
        pltpu.VMEM((512, n), BF16),
        pltpu.VMEM((K_ALL, n), BF16),
        pltpu.VMEM((256, n), BF16),
    ]


def per_device(
    single, angles, trans, left_factor, right_factor, chain, live,
    w_query, w_keyval, w_qpoints, w_kvpoints, w_pair_in, chain_bias, w_pair_out, w_bias,
    point_weight, w_out, out_gain, w_frame,
):
    vm = pl.BlockSpec(memory_space=pltpu.VMEM)
    packed = pl.pallas_call(
        pack_kernel,
        out_shape=jax.ShapeDtypeStruct((PIECE, PACK), BF16),
        in_specs=[vm] * 6,
        out_specs=vm,
        cost_estimate=pl.CostEstimate(flops=4_000_000_000, bytes_accessed=8_000_000, transcendentals=1000),
    )(single, angles, trans, right_factor, chain[None], live[None])

    own = lax.all_to_all(packed, "blk", 0, 0, tiled=True, axis_index_groups=plane_groups())
    far = lax.ppermute(own, "blk", far_perm())
    near = [own, lax.ppermute(own, "blk", CORE)]

    near[0], single_q = lax.optimization_barrier((own, single))
    *ops, fr, frt = pl.pallas_call(
        query_kernel,
        out_shape=(
            jax.ShapeDtypeStruct((256, K_ALL), BF16),
            jax.ShapeDtypeStruct((2048, 256), BF16),
            jax.ShapeDtypeStruct((320, 256), BF16),
            jax.ShapeDtypeStruct((R_ALL, PACK), BF16),
            jax.ShapeDtypeStruct((16, 128), F32),
            jax.ShapeDtypeStruct((HPAD, 144), BF16),
            jax.ShapeDtypeStruct((ROWS, 128), F32),
            jax.ShapeDtypeStruct((16, ROWS), F32),
        ),
        in_specs=[vm] * 15,
        out_specs=(vm,) * 8,
        scratch_shapes=[pltpu.VMEM((ROWS, K_ALL), F32)],
        compiler_params=pltpu.CompilerParams(vmem_limit_bytes=16 << 20),
        cost_estimate=pl.CostEstimate(flops=600_000_000, bytes_accessed=5_000_000, transcendentals=0),
    )(
        single_q, angles, trans, chain[None], live[None], left_factor, w_query.T, w_qpoints.T, w_pair_in, chain_bias[None], w_pair_out, w_bias.T,
        point_weight[None], w_keyval, w_kvpoints.T,
    )
    scratch = [pltpu.VMEM(shape, F32) for shape in STATE]
    state = pl.pallas_call(
        make_first(len(near)),
        out_shape=tuple(jax.ShapeDtypeStruct(shape, F32) for shape in STATE),
        in_specs=[vm] * (len(near) + len(ops)),
        out_specs=(vm,) * 4,
        scratch_shapes=attend_scratch(PIECE * len(near)),
        compiler_params=pltpu.CompilerParams(vmem_limit_bytes=24 << 20),
        cost_estimate=attend_cost(len(near)),
    )(*near, *ops)
    def further(taken, state):
        return pl.pallas_call(
            make_next(len(taken)),
            out_shape=tuple(jax.ShapeDtypeStruct(shape, F32) for shape in STATE),
            in_specs=[vm] * (len(taken) + len(ops) + 4),
            out_specs=(vm,) * 4,
            scratch_shapes=attend_scratch(PIECE * len(taken)),
            compiler_params=pltpu.CompilerParams(vmem_limit_bytes=20 << 20),
            cost_estimate=attend_cost(len(taken)),
        )(*taken, *ops, *state)

    far, state = lax.optimization_barrier((far, state))
    other = [lax.ppermute(far, "blk", CORE)]
    state = further([far], state)
    out, frames = pl.pallas_call(
        make_last(len(other)),
        out_shape=(
            jax.ShapeDtypeStruct((ROWS, CS), BF16),
            jax.ShapeDtypeStruct((12, ROWS), F32),
        ),
        in_specs=[vm] * (len(other) + len(ops) + 4 + 6),
        out_specs=(vm, vm),
        scratch_shapes=scratch + [pltpu.VMEM((256, 128), F32), pltpu.VMEM((ROWS, 576), F32)] + attend_scratch(PIECE * len(other)),
        compiler_params=pltpu.CompilerParams(vmem_limit_bytes=20 << 20),
        cost_estimate=attend_cost(len(other)),
    )(*other, *ops, *state, single, fr, frt, w_out, out_gain, w_frame.T)
    return out, frames


def solution(mesh):
    in_specs = (
        P("blk", None), P(None, "blk"), P(None, "blk"), P("blk", None), P("blk", None), P("blk"), P("blk"),
    ) + (P(),) * 12
    out_specs = (P("blk", None), P(None, "blk"))
    return jax.shard_map(per_device, mesh=mesh, in_specs=in_specs, out_specs=out_specs, check_vma=False)
```
